32 devices in a mesh: groups: 2 (over y), tile: 8 (over z, x), sub: 2 (over core).
Axes of the slice: x: 2, y: 2, z: 4, core: 2. Of those that a mesh axis runs over, the one named last changes fastest.
Arguments:
- features: bfloat16 [512, 128], P(('groups', 'tile')), parts along dimension 0, may hold values from -6 to 6
- weight: bfloat16 [3, 3, 48, 128], replicated, may hold values from -0.1875 to 0.1875
- out_bias: float32 [48], replicated, may hold values from -0.5 to 0.5
- band_tiles: int32 [32], P(('groups', 'tile')), parts along dimension 0, may hold values from 0 to 15, as said below
- band_width: int32 [4], P('groups'), parts along dimension 0, may hold values from 4 to 8, as said below
- cotangent: bfloat16 [32, 48, 128, 128], P(('groups', 'tile'), None, 'sub'), parts along dimension 0, may hold values from -0.29882812 to 0.29882812
Outputs:
- prediction: bfloat16 [32, 48, 128, 128], P(('groups', 'tile'), None, 'sub'), parts along dimension 0
- feature_grad: float32 [512, 128], P(('groups', 'tile')), parts along dimension 0
- weight_grad: float32 [6, 3, 48, 128], P('groups'), parts along dimension 0
- bias_grad: float32 [96], P('groups'), parts along dimension 0
The draws below stay inside these ranges and needn't reach their ends.
There are 2 independent parts, one for each index of `groups`. The reference program is written for one: setup_inputs(seed, part) draws one part's arguments, and reference() takes and returns one part's arrays. A program takes and returns all parts, laid end to end along the dimension named above; an argument that names none is the same for every part. Nothing has to cross between parts.
Inputs may be any that keep to these rules, and one draw needn't show every extreme that they name: `band_tiles`: each band tile number appears in exactly one slot; number t is tile row t // 8 at tile offset t % 8 from the diagonal. `band_width`: some tile row has width 8.
All inputs are finite; a program needn't handle non-finite values.
Results may differ from the reference program's by a relative error of at most 0.0048.
Values may be sent and summed in bfloat16 or wider, within the bound.
A program may use at most 128 MiB of HBM per device.

```python
import jax
import jax.numpy as jnp
from jax import lax

C = 128
CO = 48
RATE = 8
TILE = 128
BAND_T = 8
TPD = 2
SLOTS = 16
NB = 2
BINS = 256


def band_layout(key):
    base_key = jax.random.fold_in(key, 29)
    width_key, widest_key, tile_key, slot_key = jax.random.split(base_key, 4)
    widths = jax.random.randint(width_key, (NB,), BAND_T // 2, BAND_T + 1)
    widest = jax.random.randint(widest_key, (), 0, NB)
    widths = jnp.where(jnp.arange(NB) == widest, BAND_T, widths).astype(jnp.int32)
    tiles = jnp.arange(SLOTS, dtype=jnp.int32)
    usable = tiles % BAND_T < widths[tiles // BAND_T]
    tile_rank = jax.random.permutation(tile_key, SLOTS).astype(jnp.int32)
    tile_keys = jnp.where(usable, 0, SLOTS) + tile_rank
    tile_order = jnp.argsort(tile_keys, stable=True).astype(jnp.int32)
    slot_rank = jax.random.permutation(slot_key, SLOTS).astype(jnp.int32)
    slot_keys = jnp.where(tiles % TPD == 0, 0, SLOTS) + slot_rank
    slot_order = jnp.argsort(slot_keys, stable=True).astype(jnp.int32)
    placed = jnp.zeros((SLOTS,), jnp.int32).at[slot_order].set(tile_order)
    return (widths, placed)


def draw_band_width(key, part):
    return band_layout(key)[0]


def draw_band_tiles(key, part):
    return band_layout(key)[1]


def steps_of(key, dims, cuts, low, high):
    level, own = 1.0, jax.random.fold_in(key, 6)
    for axis_at, shards_of in cuts:
        heights = jnp.exp(jax.random.uniform(jax.random.fold_in(own, axis_at), (shards_of,), jnp.float32, low / len(cuts), high / len(cuts)))
        level = level * jnp.repeat(heights, dims[axis_at] // shards_of).reshape([-1 if axis == axis_at else 1 for axis in range(len(dims))])
    return level


def gaussian(rng, shape, width, bound, pieces=(), kind=jnp.bfloat16):
    loudness = steps_of(rng, shape, pieces, -0.22, 0.18) if pieces else 1.0
    drawn = jax.random.normal(rng, shape, jnp.float32) * width * loudness
    return jnp.minimum(jnp.maximum(drawn, -bound), bound).astype(kind)


def setup_inputs(seed: int = 0, part: int = 0) -> dict:
    seeds = jax.random.split(jax.random.key(seed), 7)
    part_splits = jax.random.split(jax.random.fold_in(seeds[6], part), 7)
    features = gaussian(part_splits[0], (BINS, C), 1.0, 6.0, ((0, 8),))
    weight = gaussian(seeds[1], (3, 3, CO, C), (9 * C) ** -0.5, 0.1875)
    out_bias = jnp.clip(jax.random.uniform(seeds[2], (CO,), jnp.float32, -0.5, 0.5), -0.5, 0.5)
    band_tiles = draw_band_tiles(jax.random.fold_in(jax.random.fold_in(seeds[6], part), 71), part)
    band_width = draw_band_width(jax.random.fold_in(jax.random.fold_in(seeds[6], part), 71), part)
    cotangent = gaussian(part_splits[5], (SLOTS, CO, TILE, TILE), 0.05, 0.29882812, ((0, 8), (2, 2)))
    return {"features": features, "weight": weight, "out_bias": out_bias, "band_tiles": band_tiles, "band_width": band_width, "cotangent": cotangent}


HIGHEST = lax.Precision.HIGHEST


def inside_bins(start_index, length, total_bins):
    positions = start_index - RATE + jnp.arange(length, dtype=jnp.int32)
    return (positions >= 0) & (positions < total_bins)


def add_rows(totals, piece, start_index):
    current = lax.dynamic_slice_in_dim(totals, start_index, piece.shape[0], 0)
    return lax.dynamic_update_slice_in_dim(totals, current + piece, start_index, 0)


def tile_terms(padded, weight, out_bias, grad_tile, row_start, col_start, total_bins):
    tile_rows = grad_tile.shape[1]
    tile_cols = grad_tile.shape[2]
    row_feat = lax.dynamic_slice_in_dim(padded, row_start, tile_rows + 2 * RATE, 0).astype(jnp.float32)
    col_feat = lax.dynamic_slice_in_dim(padded, col_start, tile_cols + 2 * RATE, 0).astype(jnp.float32)
    pair_sum = row_feat.T[:, :, None] + col_feat.T[:, None, :]
    rows_inside = inside_bins(row_start, tile_rows + 2 * RATE, total_bins)
    cols_inside = inside_bins(col_start, tile_cols + 2 * RATE, total_bins)
    active = (pair_sum > 0.0) & rows_inside[None, :, None] & cols_inside[None, None, :]
    hidden_low = lax.optimization_barrier(jnp.where(active, pair_sum, 0.0).astype(jnp.bfloat16))
    hidden = hidden_low.astype(jnp.float32)
    weight_full = weight.astype(jnp.float32)
    grad_full = grad_tile.astype(jnp.float32)
    grad_padded = jnp.pad(grad_full, ((0, 0), (2 * RATE, 2 * RATE), (2 * RATE, 2 * RATE)))
    predicted = jnp.zeros((grad_tile.shape[0], tile_rows, tile_cols), jnp.float32) + out_bias[:, None, None]
    hidden_grad = jnp.zeros(hidden.shape, jnp.float32)
    weight_rows = []
    for tap_row in range(3):
        tap_terms = []
        for tap_col in range(3):
            window = hidden[:, RATE * tap_row:RATE * tap_row + tile_rows, RATE * tap_col:RATE * tap_col + tile_cols]
            predicted = predicted + jnp.einsum("oc,cpq->opq", weight_full[tap_row, tap_col], window, precision=HIGHEST)
            tap_terms.append(jnp.einsum("cpq,opq->oc", window, grad_full, precision=HIGHEST))
            row_from = RATE * (2 - tap_row)
            col_from = RATE * (2 - tap_col)
            shifted = grad_padded[:, row_from:row_from + tile_rows + 2 * RATE, col_from:col_from + tile_cols + 2 * RATE]
            hidden_grad = hidden_grad + jnp.einsum("oc,opq->cpq", weight_full[tap_row, tap_col], shifted, precision=HIGHEST)
        weight_rows.append(jnp.stack(tap_terms))
    pair_grad = jnp.where(active, hidden_grad, 0.0)
    return (predicted.astype(jnp.bfloat16), jnp.sum(pair_grad, axis=2).T, jnp.sum(pair_grad, axis=1).T,
            jnp.stack(weight_rows), jnp.sum(grad_full, axis=(1, 2)))


def reference(features, weight, out_bias, band_tiles, band_width, cotangent):
    total_bins = features.shape[0]
    tail_bins = BAND_T * TILE
    padded = jnp.pad(features, ((RATE, RATE + tail_bins), (0, 0)))

    def one_slot(carried, inputs):
        tile_id, grad_tile = inputs
        tile_row = tile_id // BAND_T
        offset = tile_id % BAND_T
        is_valid = offset < band_width[tile_row]
        row_start = (tile_row * TILE).astype(jnp.int32)
        col_start = ((tile_row + offset) * TILE).astype(jnp.int32)

        def compute(held):
            rows_total, weight_total, bias_total = held
            predicted, row_part, col_part, weight_part, bias_part = tile_terms(
                padded, weight, out_bias, grad_tile, row_start, col_start, total_bins)
            rows_total = add_rows(rows_total, row_part, row_start)
            rows_total = add_rows(rows_total, col_part, col_start)
            return predicted, rows_total, weight_total + weight_part, bias_total + bias_part

        def skipped(held):
            return (jnp.zeros(grad_tile.shape, jnp.bfloat16), held[0], held[1], held[2])

        predicted, rows_total, weight_total, bias_total = lax.cond(is_valid, compute, skipped, carried)
        return (rows_total, weight_total, bias_total), predicted

    start_state = (jnp.zeros((total_bins + 2 * RATE + tail_bins, features.shape[1]), jnp.float32),
                   jnp.zeros(weight.shape, jnp.float32), jnp.zeros(out_bias.shape, jnp.float32))
    final_state, prediction = lax.scan(one_slot, start_state, (band_tiles, cotangent))
    rows_total, weight_total, bias_total = final_state
    return (prediction, rows_total[RATE:RATE + total_bins], weight_total, bias_total)
```

```python
import functools

import jax
import jax.numpy as jnp
from jax import lax
from jax.experimental import pallas as pl
from jax.experimental.pallas import tpu as pltpu
from jax.sharding import PartitionSpec as P

RATE = 8
TILE = 128
BAND_T = 8
FAR = -1e30
STEP = 4
MESH = pl.DeviceIdType.MESH


def gather_kernel(tiles, x_ref, out_ref, held, send_sem, recv_sem):
    me = lax.axis_index("tile")
    rows = x_ref.shape[0]
    total = tiles * rows

    def peer_of(d):
        return lax.rem(me + d, tiles)

    barrier = pltpu.get_barrier_semaphore()

    def greet(d, carry):
        pl.semaphore_signal(barrier, inc=1, device_id={"tile": peer_of(d)}, device_id_type=MESH)
        return carry

    lax.fori_loop(1, tiles, greet, 0)
    pl.semaphore_wait(barrier, tiles - 1)

    def copy_of(d):
        return pltpu.make_async_remote_copy(
            src_ref=x_ref,
            dst_ref=held.at[me],
            send_sem=send_sem.at[d],
            recv_sem=recv_sem.at[d],
            device_id={"tile": peer_of(d)},
            device_id_type=MESH,
        )

    def start(d, carry):
        copy_of(d).start()
        return carry

    lax.fori_loop(1, tiles, start, 0)
    out_ref[0:RATE, :] = jnp.full((RATE, 128), FAR, jnp.float32)
    tail = out_ref.shape[0] - RATE - total
    out_ref[RATE + total :, :] = jnp.full((tail, 128), FAR, jnp.float32)
    own = pl.multiple_of(RATE + me * rows, RATE)
    out_ref[pl.ds(own, rows), :] = x_ref[...].astype(jnp.float32)

    def finish(d, carry):
        copy_of(d).wait()
        source = lax.rem(me - d + tiles, tiles)
        at = pl.multiple_of(RATE + source * rows, RATE)
        out_ref[pl.ds(at, rows), :] = held[source].astype(jnp.float32)
        return carry

    lax.fori_loop(1, tiles, finish, 0)


def compute_kernel(
    sub_rows, tiles, chunk_rows, feat_rows, total_bins,
    ids_ref, width_ref, sub_ref,
    feat_ref, weight_ref, bias_ref, cot_ref,
    pred_ref, part_ref,
    grads, preds, col_acc, row_acc, weight_acc, bias_acc, feat_acc, flat,
):
    slot = pl.program_id(0)
    out_channels = cot_ref.shape[1]
    stacked = 3 * out_channels
    ext = sub_rows + 2 * RATE
    wide = TILE + 2 * RATE

    @pl.when(slot == 0)
    def _():
        weight_acc[...] = jnp.zeros_like(weight_acc)
        bias_acc[...] = jnp.zeros_like(bias_acc)
        feat_acc[...] = jnp.zeros_like(feat_acc)
        pad = jnp.zeros((2 * RATE, out_channels, TILE), grads.dtype)
        grads[0 : 2 * RATE] = pad
        grads[2 * RATE + sub_rows : 4 * RATE + sub_rows] = pad

    tile_id = ids_ref[slot]
    tile_row = tile_id // BAND_T
    offset = tile_id - tile_row * BAND_T
    valid = offset < width_ref[tile_row]
    row_start = pl.multiple_of(tile_row * TILE + sub_ref[0] * sub_rows, RATE)
    col_start = pl.multiple_of((tile_row + offset) * TILE, TILE)
    reaches = jnp.logical_and(valid, col_start <= total_bins)

    @pl.when(jnp.logical_not(valid))
    def _():
        pred_ref[...] = jnp.zeros_like(pred_ref)

    @pl.when(valid)
    def _():
        total = jnp.zeros((out_channels, 16, TILE), jnp.float32)
        for p in range(0, sub_rows, 16):
            total = total + cot_ref[0, :, p : p + 16, :].astype(jnp.float32)
        bias_acc[...] += jnp.sum(total, axis=1)

    @pl.when(jnp.logical_and(valid, jnp.logical_not(reaches)))
    def _():
        filled = jnp.broadcast_to(bias_ref[...][:, None, :], (out_channels, 16, TILE))
        filled = filled.astype(jnp.bfloat16)
        for p in range(0, sub_rows, 16):
            pred_ref[0, :, p : p + 16, :] = filled

    @pl.when(reaches)
    def _():
        for p in range(0, sub_rows, 16):
            block = cot_ref[0, :, p : p + 16, :].astype(jnp.float32)
            grads[2 * RATE + p : 2 * RATE + p + 16] = jnp.transpose(block, (1, 0, 2)).astype(
                grads.dtype
            )
        bias_rows = bias_ref[...]

        @pl.loop(0, sub_rows + 4 * RATE)
        def _(p):
            preds[p] = bias_rows

        col_acc[...] = jnp.zeros_like(col_acc)

        @pl.loop(0, ext // STEP)
        def _(k):
            first = k * STEP
            col_feat = feat_ref[pl.ds(col_start, wide), :]
            hidden, active, stacks = [], [], []
            for j in range(STEP):
                p = first + j
                pair = feat_ref[pl.ds(row_start + p, 1), :] + col_feat
                active.append(pair > 0.0)
                relu = jnp.maximum(pair, 0.0)
                hidden.append(
                    jnp.concatenate(
                        [relu[RATE * b : RATE * b + TILE].astype(jnp.bfloat16) for b in range(3)],
                        axis=1,
                    )
                )
                stacks.append(
                    jnp.concatenate([grads[p + RATE * (2 - a)] for a in range(3)], axis=0)
                )
            hidden_all = jnp.concatenate(hidden, axis=0)
            stack_all = jnp.concatenate(stacks, axis=1)
            weights = weight_ref[...]
            weight_acc[...] += jnp.dot(
                stack_all, hidden_all, preferred_element_type=jnp.float32
            )
            shifted = lax.dot_general(
                weights, hidden_all, (((1,), (1,)), ((), ())),
                preferred_element_type=jnp.float32,
            )
            back = lax.dot_general(
                stack_all, weights, (((0,), (0,)), ((), ())),
                preferred_element_type=jnp.float32,
            )
            gathered = jnp.zeros((wide, TILE), jnp.float32)
            low = jnp.zeros((RATE, TILE), jnp.float32)
            for j in range(STEP):
                p = first + j
                for a in range(3):
                    preds[p + RATE * (2 - a)] += shifted[
                        a * out_channels : (a + 1) * out_channels, j * TILE : (j + 1) * TILE
                    ]
                taps = [back[j * TILE : (j + 1) * TILE, b * 128 : (b + 1) * 128] for b in range(3)]
                full = (
                    jnp.concatenate([taps[0], low, low], axis=0)
                    + jnp.concatenate([low, taps[1], low], axis=0)
                    + jnp.concatenate([low, low, taps[2]], axis=0)
                )
                full = jnp.where(active[j], full, 0.0)
                gathered = gathered + full
                row_acc[pl.ds(p, 1), :] = jnp.sum(full, axis=0, keepdims=True)
            col_acc[...] += gathered

        feat_acc[pl.ds(row_start, ext), :] += row_acc[...]
        feat_acc[pl.ds(col_start, wide), :] += col_acc[...]
        for p in range(0, sub_rows, 16):
            block = preds[2 * RATE + p : 2 * RATE + p + 16]
            pred_ref[0, :, p : p + 16, :] = jnp.transpose(block, (1, 0, 2)).astype(jnp.bfloat16)

    @pl.when(slot == pl.num_programs(0) - 1)
    def _():
        flat[...] = jnp.zeros_like(flat)
        for a in range(3):
            for b in range(3):
                at = (a * 3 + b) * out_channels
                flat[at : at + out_channels, :] = weight_acc[
                    a * out_channels : (a + 1) * out_channels, b * 128 : (b + 1) * 128
                ]
        flat[3 * stacked : 3 * stacked + out_channels, :] = bias_acc[...]

        @pl.loop(0, tiles)
        def _(t):
            for half in range(2):
                start = pl.multiple_of(RATE + (t * 2 + half) * feat_rows, RATE)
                part_ref[half, t, 0:feat_rows, :] = feat_acc[pl.ds(start, feat_rows), :]
                at = pl.multiple_of((half * tiles + t) * chunk_rows, RATE)
                part_ref[half, t, feat_rows:, :] = flat[pl.ds(at, chunk_rows), :]


def reduce_kernel(
    tiles, feat_rows, part_ref, feat_ref, out_ref,
    from_core, comb, from_tiles, own_feat, gathered,
    core_sem, scatter_sem, gather_sem, forward_sem, feat_sem,
):
    me = lax.axis_index("tile")
    sub = lax.axis_index("sub")
    other = 1 - sub

    def peer_of(d):
        return lax.rem(me + d, tiles)

    def source_of(d):
        return lax.rem(me - d + tiles, tiles)

    def remote(src, dst, sems, where):
        return pltpu.make_async_remote_copy(
            src_ref=src, dst_ref=dst, send_sem=sems[0], recv_sem=sems[1],
            device_id=where, device_id_type=MESH,
        )

    barrier = pltpu.get_barrier_semaphore()
    pl.semaphore_signal(barrier, inc=1, device_id={"sub": other}, device_id_type=MESH)

    def greet(d, carry):
        pl.semaphore_signal(barrier, inc=1, device_id={"tile": peer_of(d)}, device_id_type=MESH)
        return carry

    lax.fori_loop(1, tiles, greet, 0)
    pl.semaphore_wait(barrier, tiles)

    core = remote(
        part_ref.at[other], from_core, (core_sem.at[0], core_sem.at[1]), {"sub": other}
    )
    core.start()
    core.wait()
    comb[...] = part_ref[sub] + from_core[...]

    def scatter_of(d):
        return remote(
            comb.at[peer_of(d)], from_tiles.at[d],
            (scatter_sem.at[0, d], scatter_sem.at[1, d]), {"tile": peer_of(d)},
        )

    def scatter_start(d, carry):
        scatter_of(d).start()
        return carry

    lax.fori_loop(1, tiles, scatter_start, 0)

    def scatter_add(d, total):
        scatter_of(d).wait()
        return total + from_tiles[d]

    total = lax.fori_loop(1, tiles, scatter_add, comb[me])
    own_feat[sub] = total[0:feat_rows]
    gathered[sub, me] = total[feat_rows:]

    def gather_of(d):
        return remote(
            gathered.at[sub, me], gathered.at[sub, me],
            (gather_sem.at[0, d], gather_sem.at[1, d]), {"tile": peer_of(d)},
        )

    def forward_of(d):
        source = source_of(d)
        return remote(
            gathered.at[sub, source], gathered.at[sub, source],
            (forward_sem.at[0, d], forward_sem.at[1, d]), {"sub": other},
        )

    def gather_start(d, carry):
        gather_of(d).start()
        return carry

    lax.fori_loop(1, tiles, gather_start, 0)
    feat_copy = remote(
        own_feat.at[sub], own_feat.at[sub], (feat_sem.at[0], feat_sem.at[1]), {"sub": other}
    )
    feat_copy.start()
    forward_of(0).start()

    def forward(d, carry):
        gather_of(d).wait()
        forward_of(d).start()
        return carry

    lax.fori_loop(1, tiles, forward, 0)

    def forward_end(d, carry):
        forward_of(d).wait()
        return carry

    lax.fori_loop(0, tiles, forward_end, 0)
    feat_copy.wait()
    feat_ref[...] = own_feat[...]
    out_ref[...] = gathered[...]


def on_device(tiles, subs, features, weight, out_bias, band_tiles, band_width, cotangent):
    rows, channels = features.shape
    slots, out_channels, sub_rows, _ = cotangent.shape
    total_bins = tiles * rows
    stacked = 3 * out_channels
    vmem = pl.BlockSpec(memory_space=pltpu.VMEM)
    padded = pl.pallas_call(
        functools.partial(gather_kernel, tiles),
        out_shape=jax.ShapeDtypeStruct((total_bins + TILE + 2 * RATE, channels), jnp.float32),
        in_specs=[vmem],
        out_specs=vmem,
        scratch_shapes=[
            pltpu.VMEM((tiles, rows, channels), features.dtype),
            pltpu.SemaphoreType.DMA((tiles,)),
            pltpu.SemaphoreType.DMA((tiles,)),
        ],
        compiler_params=pltpu.CompilerParams(collective_id=0, has_side_effects=True),
    )(features)

    feat_rows = rows // 2
    flat_rows = 3 * stacked + out_channels
    chunk_rows = -(-flat_rows // (2 * tiles * RATE)) * RATE
    part_rows = feat_rows + chunk_rows
    weights = jnp.transpose(weight, (0, 2, 1, 3)).reshape(stacked, 3 * channels)
    bias_rows = jnp.broadcast_to(out_bias[:, None], (out_channels, TILE))
    sub_index = lax.axis_index("sub").astype(jnp.int32).reshape(1)
    ext = sub_rows + 2 * RATE
    wide = TILE + 2 * RATE
    padded_rows = total_bins + wide

    def whole(shape):
        return pl.BlockSpec(shape, lambda i, *_: (0,) * len(shape))

    block = pl.BlockSpec((1, out_channels, sub_rows, TILE), lambda i, *_: (i, 0, 0, 0))
    prediction, part = pl.pallas_call(
        functools.partial(compute_kernel, sub_rows, tiles, chunk_rows, feat_rows, total_bins),
        out_shape=(
            jax.ShapeDtypeStruct(cotangent.shape, jnp.bfloat16),
            jax.ShapeDtypeStruct((2, tiles, part_rows, channels), jnp.float32),
        ),
        grid_spec=pltpu.PrefetchScalarGridSpec(
            num_scalar_prefetch=3,
            grid=(slots,),
            in_specs=[
                whole((padded_rows, channels)),
                whole((stacked, 3 * channels)),
                whole((out_channels, TILE)),
                block,
            ],
            out_specs=[block, whole((2, tiles, part_rows, channels))],
            scratch_shapes=[
                pltpu.VMEM((sub_rows + 4 * RATE, out_channels, TILE), jnp.bfloat16),
                pltpu.VMEM((sub_rows + 4 * RATE, out_channels, TILE), jnp.float32),
                pltpu.VMEM((wide, channels), jnp.float32),
                pltpu.VMEM((ext, channels), jnp.float32),
                pltpu.VMEM((stacked, 3 * channels), jnp.float32),
                pltpu.VMEM((out_channels, TILE), jnp.float32),
                pltpu.VMEM((padded_rows, channels), jnp.float32),
                pltpu.VMEM((2 * tiles * chunk_rows, channels), jnp.float32),
            ],
        ),
        compiler_params=pltpu.CompilerParams(vmem_limit_bytes=48 << 20),
    )(band_tiles, band_width, sub_index, padded, weights, bias_rows, cotangent)

    feature_grad, sums = pl.pallas_call(
        functools.partial(reduce_kernel, tiles, feat_rows),
        out_shape=(
            jax.ShapeDtypeStruct((2, feat_rows, channels), jnp.float32),
            jax.ShapeDtypeStruct((2, tiles, chunk_rows, channels), jnp.float32),
        ),
        in_specs=[vmem],
        out_specs=(vmem, vmem),
        scratch_shapes=[
            pltpu.VMEM((tiles, part_rows, channels), jnp.float32),
            pltpu.VMEM((tiles, part_rows, channels), jnp.float32),
            pltpu.VMEM((tiles, part_rows, channels), jnp.float32),
            pltpu.VMEM((2, feat_rows, channels), jnp.float32),
            pltpu.VMEM((2, tiles, chunk_rows, channels), jnp.float32),
            pltpu.SemaphoreType.DMA((2,)),
            pltpu.SemaphoreType.DMA((2, tiles)),
            pltpu.SemaphoreType.DMA((2, tiles)),
            pltpu.SemaphoreType.DMA((2, tiles)),
            pltpu.SemaphoreType.DMA((2,)),
        ],
        compiler_params=pltpu.CompilerParams(
            collective_id=1, has_side_effects=True, vmem_limit_bytes=48 << 20
        ),
    )(part)
    sums = sums.reshape(-1, channels)
    weight_grad = sums[: 3 * stacked].reshape(weight.shape)
    bias_grad = jnp.sum(sums[3 * stacked : flat_rows], axis=1)
    return (prediction, feature_grad.reshape(rows, channels), weight_grad, bias_grad)


def solution(mesh):
    in_specs = (
        P(("groups", "tile"), None),
        P(),
        P(),
        P(("groups", "tile")),
        P("groups"),
        P(("groups", "tile"), None, "sub", None),
    )
    out_specs = (
        P(("groups", "tile"), None, "sub", None),
        P(("groups", "tile"), None),
        P("groups", None, None, None),
        P("groups"),
    )
    return jax.shard_map(
        functools.partial(on_device, mesh.shape["tile"], mesh.shape["sub"]),
        mesh=mesh, in_specs=in_specs, out_specs=out_specs, check_vma=False,
    )
```

```python
import functools

import jax
import jax.numpy as jnp
from jax import lax
from jax.experimental import pallas as pl
from jax.experimental.pallas import tpu as pltpu
from jax.sharding import PartitionSpec as P

RATE = 8
TILE = 128
BAND_T = 8
FAR = -1e30
STEP = 4
MESH = pl.DeviceIdType.MESH


def gather_kernel(tiles, x_ref, out_ref, held, send_sem, recv_sem):
    me = lax.axis_index("tile")
    rows = x_ref.shape[0]
    total = tiles * rows

    def peer_of(d):
        return lax.rem(me + d, tiles)

    barrier = pltpu.get_barrier_semaphore()

    def greet(d, carry):
        pl.semaphore_signal(barrier, inc=1, device_id={"tile": peer_of(d)}, device_id_type=MESH)
        return carry

    lax.fori_loop(1, tiles, greet, 0)
    pl.semaphore_wait(barrier, tiles - 1)

    def copy_of(d):
        return pltpu.make_async_remote_copy(
            src_ref=x_ref,
            dst_ref=held.at[me],
            send_sem=send_sem.at[d],
            recv_sem=recv_sem.at[d],
            device_id={"tile": peer_of(d)},
            device_id_type=MESH,
        )

    def start(d, carry):
        copy_of(d).start()
        return carry

    lax.fori_loop(1, tiles, start, 0)
    out_ref[0:RATE, :] = jnp.full((RATE, 128), FAR, jnp.float32)
    tail = out_ref.shape[0] - RATE - total
    out_ref[RATE + total :, :] = jnp.full((tail, 128), FAR, jnp.float32)
    own = pl.multiple_of(RATE + me * rows, RATE)
    out_ref[pl.ds(own, rows), :] = x_ref[...].astype(jnp.float32)

    def finish(d, carry):
        copy_of(d).wait()
        source = lax.rem(me - d + tiles, tiles)
        at = pl.multiple_of(RATE + source * rows, RATE)
        out_ref[pl.ds(at, rows), :] = held[source].astype(jnp.float32)
        return carry

    lax.fori_loop(1, tiles, finish, 0)


def compute_kernel(
    sub_rows, tiles, chunk_rows, feat_rows, total_bins,
    ids_hbm, width_hbm, feat_ref, weight_in, bias_in, cot_hbm,
    pred_ref, part_ref,
    ids_ref, width_ref, cots, weight_ref, bias_ref,
    grads, preds, col_acc, row_acc, weight_acc, bias_acc, feat_acc, flat,
    table_sem, cot_sem,
):
    slot = pl.program_id(0)
    slots, out_channels = cots.shape[:2]
    cot_ref = cots.at[pl.ds(slot, 1)]
    sub = lax.axis_index("sub")

    def cot_copy(at):
        return pltpu.make_async_copy(cot_hbm.at[at], cots.at[at], cot_sem.at[at])

    stacked = 3 * out_channels
    ext = sub_rows + 2 * RATE
    wide = TILE + 2 * RATE

    @pl.when(slot == 0)
    def _():
        ids_copy = pltpu.make_async_copy(ids_hbm, ids_ref, table_sem.at[0])
        width_copy = pltpu.make_async_copy(width_hbm, width_ref, table_sem.at[1])
        ids_copy.start()
        width_copy.start()
        for at in range(slots):
            cot_copy(at).start()
        for a in range(3):
            for b in range(3):
                weight_ref[
                    a * out_channels : (a + 1) * out_channels, b * 128 : (b + 1) * 128
                ] = weight_in[a, b]
        bias_ref[...] = jnp.transpose(
            jnp.broadcast_to(bias_in[...], (TILE, out_channels)), (1, 0)
        )
        weight_acc[...] = jnp.zeros_like(weight_acc)
        bias_acc[...] = jnp.zeros_like(bias_acc)
        feat_acc[...] = jnp.zeros_like(feat_acc)
        pad = jnp.zeros((2 * RATE, out_channels, TILE), grads.dtype)
        grads[0 : 2 * RATE] = pad
        grads[2 * RATE + sub_rows : 4 * RATE + sub_rows] = pad
        ids_copy.wait()
        width_copy.wait()

    cot_copy(slot).wait()

    tile_id = ids_ref[slot]
    tile_row = tile_id // BAND_T
    offset = tile_id - tile_row * BAND_T
    valid = offset < width_ref[tile_row]
    row_start = pl.multiple_of(tile_row * TILE + sub * sub_rows, RATE)
    col_start = pl.multiple_of((tile_row + offset) * TILE, TILE)
    reaches = jnp.logical_and(valid, col_start <= total_bins)

    @pl.when(jnp.logical_not(valid))
    def _():
        pred_ref[...] = jnp.zeros_like(pred_ref)

    @pl.when(valid)
    def _():
        total = jnp.zeros((out_channels, 16, TILE), jnp.float32)
        for p in range(0, sub_rows, 16):
            total = total + cot_ref[0, :, p : p + 16, :].astype(jnp.float32)
        bias_acc[...] += jnp.sum(total, axis=1)

    @pl.when(jnp.logical_and(valid, jnp.logical_not(reaches)))
    def _():
        filled = jnp.broadcast_to(bias_ref[...][:, None, :], (out_channels, 16, TILE))
        filled = filled.astype(jnp.bfloat16)
        for p in range(0, sub_rows, 16):
            pred_ref[0, :, p : p + 16, :] = filled

    @pl.when(reaches)
    def _():
        for p in range(0, sub_rows, 16):
            block = cot_ref[0, :, p : p + 16, :].astype(jnp.float32)
            grads[2 * RATE + p : 2 * RATE + p + 16] = jnp.transpose(block, (1, 0, 2)).astype(
                grads.dtype
            )
        bias_rows = bias_ref[...]

        @pl.loop(0, sub_rows + 4 * RATE)
        def _(p):
            preds[p] = bias_rows

        col_acc[...] = jnp.zeros_like(col_acc)

        def sweep(k, columns):
            first = k * STEP
            taps_wide = columns * 128
            col_feat = feat_ref[pl.ds(col_start, wide), :]
            hidden, active, stacks = [], [], []
            for j in range(STEP):
                p = first + j
                pair = feat_ref[pl.ds(row_start + p, 1), :] + col_feat
                active.append(pair > 0.0)
                relu = jnp.maximum(pair, 0.0)
                hidden.append(
                    jnp.concatenate(
                        [relu[RATE * b : RATE * b + TILE].astype(jnp.bfloat16) for b in range(columns)],
                        axis=1,
                    )
                )
                stacks.append(
                    jnp.concatenate([grads[p + RATE * (2 - a)] for a in range(3)], axis=0)
                )
            hidden_all = jnp.concatenate(hidden, axis=0)
            stack_all = jnp.concatenate(stacks, axis=1)
            weights = weight_ref[:, 0:taps_wide]
            weight_acc[:, 0:taps_wide] += jnp.dot(
                stack_all, hidden_all, preferred_element_type=jnp.float32
            )
            shifted = lax.dot_general(
                weights, hidden_all, (((1,), (1,)), ((), ())),
                preferred_element_type=jnp.float32,
            )
            back = lax.dot_general(
                stack_all, weights, (((0,), (0,)), ((), ())),
                preferred_element_type=jnp.float32,
            )
            gathered = jnp.zeros((wide, TILE), jnp.float32)
            low = jnp.zeros((RATE, TILE), jnp.float32)
            for j in range(STEP):
                p = first + j
                for a in range(3):
                    preds[p + RATE * (2 - a)] += shifted[
                        a * out_channels : (a + 1) * out_channels, j * TILE : (j + 1) * TILE
                    ]
                full = jnp.zeros((wide, TILE), jnp.float32)
                for b in range(columns):
                    tap = back[j * TILE : (j + 1) * TILE, b * 128 : (b + 1) * 128]
                    full = full + jnp.concatenate([low] * b + [tap] + [low] * (2 - b), axis=0)
                full = jnp.where(active[j], full, 0.0)
                gathered = gathered + full
                row_acc[pl.ds(p, 1), :] = jnp.sum(full, axis=0, keepdims=True)
            col_acc[...] += gathered

        @pl.when(col_start < total_bins)
        def _():
            pl.loop(0, ext // STEP)(lambda k: sweep(k, 3))

        @pl.when(col_start >= total_bins)
        def _():
            pl.loop(0, ext // STEP)(lambda k: sweep(k, 1))

        feat_acc[pl.ds(row_start, ext), :] += row_acc[...]
        feat_acc[pl.ds(col_start, wide), :] += col_acc[...]
        for p in range(0, sub_rows, 16):
            block = preds[2 * RATE + p : 2 * RATE + p + 16]
            pred_ref[0, :, p : p + 16, :] = jnp.transpose(block, (1, 0, 2)).astype(jnp.bfloat16)

    @pl.when(slot == pl.num_programs(0) - 1)
    def _():
        flat[...] = jnp.zeros_like(flat)
        for a in range(3):
            for b in range(3):
                at = (a * 3 + b) * out_channels
                flat[at : at + out_channels, :] = weight_acc[
                    a * out_channels : (a + 1) * out_channels, b * 128 : (b + 1) * 128
                ]
        flat[3 * stacked : 3 * stacked + out_channels, :] = bias_acc[...]

        @pl.loop(0, tiles)
        def _(t):
            for half in range(2):
                start = pl.multiple_of(RATE + (t * 2 + half) * feat_rows, RATE)
                part_ref[half, t, 0:feat_rows, :] = feat_acc[pl.ds(start, feat_rows), :]
                at = pl.multiple_of((half * tiles + t) * chunk_rows, RATE)
                part_ref[half, t, feat_rows:, :] = flat[pl.ds(at, chunk_rows), :]


def reduce_kernel(
    tiles, feat_rows, part_ref, feat_ref, out_ref,
    from_core, comb, from_tiles, sending, own_feat, gathered,
    core_sem, scatter_sem, gather_sem, forward_sem, feat_sem, load_sem,
):
    me = lax.axis_index("tile")
    sub = lax.axis_index("sub")
    other = 1 - sub

    def peer_of(d):
        return lax.rem(me + d, tiles)

    def source_of(d):
        return lax.rem(me - d + tiles, tiles)

    def remote(src, dst, sems, where):
        return pltpu.make_async_remote_copy(
            src_ref=src, dst_ref=dst, send_sem=sems[0], recv_sem=sems[1],
            device_id=where, device_id_type=MESH,
        )

    load = pltpu.make_async_copy(part_ref.at[sub], comb, load_sem)
    load.start()
    barrier = pltpu.get_barrier_semaphore()
    pl.semaphore_signal(barrier, inc=1, device_id={"sub": other}, device_id_type=MESH)

    def greet(d, carry):
        pl.semaphore_signal(barrier, inc=1, device_id={"tile": peer_of(d)}, device_id_type=MESH)
        return carry

    lax.fori_loop(1, tiles, greet, 0)
    pl.semaphore_wait(barrier, tiles)

    core = remote(
        part_ref.at[other], from_core, (core_sem.at[0], core_sem.at[1]), {"sub": other}
    )
    core.start()
    load.wait()
    core.wait()
    comb[...] += from_core[...]
    sending[...] = comb[...].astype(sending.dtype)

    def scatter_of(d):
        return remote(
            sending.at[peer_of(d)], from_tiles.at[d],
            (scatter_sem.at[0, d], scatter_sem.at[1, d]), {"tile": peer_of(d)},
        )

    def scatter_start(d, carry):
        scatter_of(d).start()
        return carry

    lax.fori_loop(1, tiles, scatter_start, 0)

    def scatter_add(d, total):
        scatter_of(d).wait()
        return total + from_tiles[d].astype(jnp.float32)

    total = lax.fori_loop(1, tiles, scatter_add, comb[me])
    own_feat[sub] = total[0:feat_rows]
    gathered[sub, me] = total[feat_rows:].astype(gathered.dtype)

    def gather_of(d):
        return remote(
            gathered.at[sub, me], gathered.at[sub, me],
            (gather_sem.at[0, d], gather_sem.at[1, d]), {"tile": peer_of(d)},
        )

    def forward_of(d):
        source = source_of(d)
        return remote(
            gathered.at[sub, source], gathered.at[sub, source],
            (forward_sem.at[0, d], forward_sem.at[1, d]), {"sub": other},
        )

    def gather_start(d, carry):
        gather_of(d).start()
        return carry

    lax.fori_loop(1, tiles, gather_start, 0)
    feat_copy = remote(
        own_feat.at[sub], own_feat.at[sub], (feat_sem.at[0], feat_sem.at[1]), {"sub": other}
    )
    feat_copy.start()
    forward_of(0).start()

    def forward(d, carry):
        gather_of(d).wait()
        forward_of(d).start()
        return carry

    lax.fori_loop(1, tiles, forward, 0)

    def forward_end(d, carry):
        forward_of(d).wait()
        return carry

    lax.fori_loop(0, tiles, forward_end, 0)
    feat_copy.wait()
    feat_ref[...] = own_feat[...]
    out_ref[...] = gathered[...]


def finish_kernel(weight_rows, feat_in, sums_in, feat_ref, weight_ref, bias_ref):
    feat_ref[...] = feat_in[...].reshape(feat_ref.shape)
    sums = sums_in[...].astype(jnp.float32).reshape(-1, feat_ref.shape[1])
    weight_ref[...] = sums[:weight_rows]
    bias = sums[weight_rows : weight_rows + bias_ref.shape[1]]
    bias_ref[...] = jnp.sum(jnp.transpose(bias, (1, 0)), axis=0, keepdims=True)


def on_device(tiles, subs, features, weight, out_bias, band_tiles, band_width, cotangent):
    rows, channels = features.shape
    slots, out_channels, sub_rows, _ = cotangent.shape
    total_bins = tiles * rows
    stacked = 3 * out_channels
    vmem = pl.BlockSpec(memory_space=pltpu.VMEM)
    padded = pl.pallas_call(
        functools.partial(gather_kernel, tiles),
        out_shape=jax.ShapeDtypeStruct((total_bins + TILE + 2 * RATE, channels), jnp.float32),
        in_specs=[vmem],
        out_specs=vmem,
        scratch_shapes=[
            pltpu.VMEM((tiles, rows, channels), features.dtype),
            pltpu.SemaphoreType.DMA((tiles,)),
            pltpu.SemaphoreType.DMA((tiles,)),
        ],
        compiler_params=pltpu.CompilerParams(
            collective_id=0, has_side_effects=True, vmem_limit_bytes=64 << 20
        ),
    )(features)

    feat_rows = rows // 2
    flat_rows = 3 * stacked + out_channels
    chunk_rows = -(-flat_rows // (2 * tiles * 16)) * 16
    part_rows = feat_rows + chunk_rows
    ext = sub_rows + 2 * RATE
    wide = TILE + 2 * RATE
    padded_rows = total_bins + wide

    def whole(shape):
        return pl.BlockSpec(shape, lambda i, *_: (0,) * len(shape))

    hbm = pl.BlockSpec(memory_space=pltpu.HBM)
    block = pl.BlockSpec((1, out_channels, sub_rows, TILE), lambda i, *_: (i, 0, 0, 0))
    prediction, part = pl.pallas_call(
        functools.partial(compute_kernel, sub_rows, tiles, chunk_rows, feat_rows, total_bins),
        out_shape=(
            jax.ShapeDtypeStruct(cotangent.shape, jnp.bfloat16),
            jax.ShapeDtypeStruct((2, tiles, part_rows, channels), jnp.float32),
        ),
        grid_spec=pltpu.PrefetchScalarGridSpec(
            num_scalar_prefetch=0,
            grid=(slots,),
            in_specs=[
                hbm,
                hbm,
                whole((padded_rows, channels)),
                whole(weight.shape),
                whole((1, out_channels)),
                hbm,
            ],
            out_specs=[block, whole((2, tiles, part_rows, channels))],
            scratch_shapes=[
                pltpu.SMEM(band_tiles.shape, jnp.int32),
                pltpu.SMEM(band_width.shape, jnp.int32),
                pltpu.VMEM(cotangent.shape, cotangent.dtype),
                pltpu.VMEM((stacked, 3 * channels), weight.dtype),
                pltpu.VMEM((out_channels, TILE), jnp.float32),
                pltpu.VMEM((sub_rows + 4 * RATE, out_channels, TILE), jnp.bfloat16),
                pltpu.VMEM((sub_rows + 4 * RATE, out_channels, TILE), jnp.float32),
                pltpu.VMEM((wide, channels), jnp.float32),
                pltpu.VMEM((ext, channels), jnp.float32),
                pltpu.VMEM((stacked, 3 * channels), jnp.float32),
                pltpu.VMEM((out_channels, TILE), jnp.float32),
                pltpu.VMEM((padded_rows, channels), jnp.float32),
                pltpu.VMEM((2 * tiles * chunk_rows, channels), jnp.float32),
                pltpu.SemaphoreType.DMA((2,)),
                pltpu.SemaphoreType.DMA((slots,)),
            ],
        ),
        compiler_params=pltpu.CompilerParams(vmem_limit_bytes=64 << 20),
    )(band_tiles, band_width, padded, weight, out_bias.reshape(1, out_channels), cotangent)

    feature_grad, sums = pl.pallas_call(
        functools.partial(reduce_kernel, tiles, feat_rows),
        out_shape=(
            jax.ShapeDtypeStruct((2, feat_rows, channels), jnp.float32),
            jax.ShapeDtypeStruct((2, tiles, chunk_rows, channels), jnp.bfloat16),
        ),
        in_specs=[hbm],
        out_specs=(vmem, vmem),
        scratch_shapes=[
            pltpu.VMEM((tiles, part_rows, channels), jnp.float32),
            pltpu.VMEM((tiles, part_rows, channels), jnp.float32),
            pltpu.VMEM((tiles, part_rows, channels), jnp.bfloat16),
            pltpu.VMEM((tiles, part_rows, channels), jnp.bfloat16),
            pltpu.VMEM((2, feat_rows, channels), jnp.float32),
            pltpu.VMEM((2, tiles, chunk_rows, channels), jnp.bfloat16),
            pltpu.SemaphoreType.DMA((2,)),
            pltpu.SemaphoreType.DMA((2, tiles)),
            pltpu.SemaphoreType.DMA((2, tiles)),
            pltpu.SemaphoreType.DMA((2, tiles)),
            pltpu.SemaphoreType.DMA((2,)),
            pltpu.SemaphoreType.DMA,
        ],
        compiler_params=pltpu.CompilerParams(
            collective_id=1, has_side_effects=True, vmem_limit_bytes=(64 << 20) - (380 << 10)
        ),
    )(part)
    feature_grad, weight_grad, bias_grad = pl.pallas_call(
        functools.partial(finish_kernel, 3 * stacked),
        out_shape=(
            jax.ShapeDtypeStruct((rows, channels), jnp.float32),
            jax.ShapeDtypeStruct((3 * stacked, channels), jnp.float32),
            jax.ShapeDtypeStruct((1, out_channels), jnp.float32),
        ),
        in_specs=[vmem, vmem],
        out_specs=(vmem, vmem, vmem),
        compiler_params=pltpu.CompilerParams(vmem_limit_bytes=64 << 20),
    )(feature_grad, sums)
    return (
        prediction,
        feature_grad,
        weight_grad.reshape(weight.shape),
        bias_grad.reshape(out_channels),
    )


def solution(mesh):
    in_specs = (
        P(("groups", "tile"), None),
        P(),
        P(),
        P(("groups", "tile")),
        P("groups"),
        P(("groups", "tile"), None, "sub", None),
    )
    out_specs = (
        P(("groups", "tile"), None, "sub", None),
        P(("groups", "tile"), None),
        P("groups", None, None, None),
        P("groups"),
    )
    return jax.shard_map(
        functools.partial(on_device, mesh.shape["tile"], mesh.shape["sub"]),
        mesh=mesh, in_specs=in_specs, out_specs=out_specs, check_vma=False,
    )
```

```python
import functools

import jax
import jax.numpy as jnp
from jax import lax
from jax.experimental import pallas as pl
from jax.experimental.pallas import tpu as pltpu
from jax.sharding import PartitionSpec as P

RATE = 8
TILE = 128
BAND_T = 8
FAR = -1e30
STEP = 16
MESH = pl.DeviceIdType.MESH


def gather_kernel(tiles, x_ref, out_ref, held, send_sem, recv_sem):
    me = lax.axis_index("tile")
    rows = x_ref.shape[0]
    total = tiles * rows

    def peer_of(d):
        return lax.rem(me + d, tiles)

    barrier = pltpu.get_barrier_semaphore()

    def greet(d, carry):
        pl.semaphore_signal(barrier, inc=1, device_id={"tile": peer_of(d)}, device_id_type=MESH)
        return carry

    lax.fori_loop(1, tiles, greet, 0)
    pl.semaphore_wait(barrier, tiles - 1)

    def copy_of(d):
        return pltpu.make_async_remote_copy(
            src_ref=x_ref,
            dst_ref=held.at[me],
            send_sem=send_sem.at[d],
            recv_sem=recv_sem.at[d],
            device_id={"tile": peer_of(d)},
            device_id_type=MESH,
        )

    def start(d, carry):
        copy_of(d).start()
        return carry

    lax.fori_loop(1, tiles, start, 0)
    out_ref[0:RATE, :] = jnp.full((RATE, 128), FAR, jnp.float32)
    tail = out_ref.shape[0] - RATE - total
    out_ref[RATE + total :, :] = jnp.full((tail, 128), FAR, jnp.float32)
    own = pl.multiple_of(RATE + me * rows, RATE)
    out_ref[pl.ds(own, rows), :] = x_ref[...].astype(jnp.float32)

    def finish(d, carry):
        copy_of(d).wait()
        source = lax.rem(me - d + tiles, tiles)
        at = pl.multiple_of(RATE + source * rows, RATE)
        out_ref[pl.ds(at, rows), :] = held[source].astype(jnp.float32)
        return carry

    lax.fori_loop(1, tiles, finish, 0)


def compute_kernel(
    sub_rows, tiles, chunk_rows, feat_rows, total_bins,
    ids_hbm, width_hbm, feat_ref, weight_in, bias_in, cot_hbm,
    pred_ref, part_ref,
    ids_ref, width_ref, cots, weight_ref, bias_ref,
    grads, preds, col_acc, row_acc, weight_acc, bias_acc, feat_acc, flat,
    table_sem, cot_sem,
):
    slot = pl.program_id(0)
    slots, out_channels = cots.shape[:2]
    cot_ref = cots.at[pl.ds(slot, 1)]
    sub = lax.axis_index("sub")

    def cot_copy(at):
        return pltpu.make_async_copy(cot_hbm.at[at], cots.at[at], cot_sem.at[at])

    stacked = 3 * out_channels
    ext = sub_rows + 2 * RATE
    wide = TILE + 2 * RATE

    @pl.when(slot == 0)
    def _():
        ids_copy = pltpu.make_async_copy(ids_hbm, ids_ref, table_sem.at[0])
        width_copy = pltpu.make_async_copy(width_hbm, width_ref, table_sem.at[1])
        ids_copy.start()
        width_copy.start()
        for at in range(slots):
            cot_copy(at).start()
        for a in range(3):
            for b in range(3):
                weight_ref[
                    a * out_channels : (a + 1) * out_channels, b * 128 : (b + 1) * 128
                ] = weight_in[a, b]
        bias_ref[...] = jnp.transpose(
            jnp.broadcast_to(bias_in[...], (TILE, out_channels)), (1, 0)
        )
        weight_acc[...] = jnp.zeros_like(weight_acc)
        bias_acc[...] = jnp.zeros_like(bias_acc)
        feat_acc[...] = jnp.zeros_like(feat_acc)
        pad = jnp.zeros((2 * RATE, out_channels, TILE), grads.dtype)
        grads[0 : 2 * RATE] = pad
        grads[2 * RATE + sub_rows : 4 * RATE + sub_rows] = pad
        ids_copy.wait()
        width_copy.wait()

    cot_copy(slot).wait()

    tile_id = ids_ref[slot]
    tile_row = tile_id // BAND_T
    offset = tile_id - tile_row * BAND_T
    valid = offset < width_ref[tile_row]
    row_start = pl.multiple_of(tile_row * TILE + sub * sub_rows, RATE)
    col_start = pl.multiple_of((tile_row + offset) * TILE, TILE)
    reaches = jnp.logical_and(valid, col_start <= total_bins)

    @pl.when(jnp.logical_not(valid))
    def _():
        pred_ref[...] = jnp.zeros_like(pred_ref)

    @pl.when(valid)
    def _():
        total = jnp.zeros((out_channels, 16, TILE), jnp.float32)
        for p in range(0, sub_rows, 16):
            total = total + cot_ref[0, :, p : p + 16, :].astype(jnp.float32)
        bias_acc[...] += jnp.sum(total, axis=1)

    @pl.when(jnp.logical_and(valid, jnp.logical_not(reaches)))
    def _():
        filled = jnp.broadcast_to(bias_ref[...][:, None, :], (out_channels, 16, TILE))
        filled = filled.astype(jnp.bfloat16)
        for p in range(0, sub_rows, 16):
            pred_ref[0, :, p : p + 16, :] = filled

    @pl.when(reaches)
    def _():
        for p in range(0, sub_rows, 16):
            block = cot_ref[0, :, p : p + 16, :].astype(jnp.float32)
            grads[2 * RATE + p : 2 * RATE + p + 16] = jnp.transpose(block, (1, 0, 2)).astype(
                grads.dtype
            )
        bias_rows = bias_ref[...]

        @pl.loop(0, sub_rows + 4 * RATE)
        def _(p):
            preds[p] = bias_rows

        col_acc[...] = jnp.zeros_like(col_acc)

        def sweep(k, columns):
            first = k * STEP
            taps_wide = columns * 128
            col_feat = feat_ref[pl.ds(col_start, wide), :]
            hidden, active, stacks = [], [], []
            for j in range(STEP):
                p = first + j
                pair = feat_ref[pl.ds(row_start + p, 1), :] + col_feat
                active.append(pair > 0.0)
                relu = jnp.maximum(pair, 0.0)
                hidden.append(
                    jnp.concatenate(
                        [relu[RATE * b : RATE * b + TILE].astype(jnp.bfloat16) for b in range(columns)],
                        axis=1,
                    )
                )
                stacks.append(
                    jnp.concatenate([grads[p + RATE * (2 - a)] for a in range(3)], axis=0)
                )
            hidden_all = jnp.concatenate(hidden, axis=0)
            stack_all = jnp.concatenate(stacks, axis=1)
            weights = weight_ref[:, 0:taps_wide]
            weight_acc[:, 0:taps_wide] += jnp.dot(
                stack_all, hidden_all, preferred_element_type=jnp.float32
            )
            shifted = lax.dot_general(
                weights, hidden_all, (((1,), (1,)), ((), ())),
                preferred_element_type=jnp.float32,
            )
            back = lax.dot_general(
                stack_all, weights, (((0,), (0,)), ((), ())),
                preferred_element_type=jnp.float32,
            )
            gathered = jnp.zeros((wide, TILE), jnp.float32)
            low = jnp.zeros((RATE, TILE), jnp.float32)
            for j in range(STEP):
                p = first + j
                for a in range(3):
                    preds[p + RATE * (2 - a)] += shifted[
                        a * out_channels : (a + 1) * out_channels, j * TILE : (j + 1) * TILE
                    ]
                full = jnp.zeros((wide, TILE), jnp.float32)
                for b in range(columns):
                    tap = back[j * TILE : (j + 1) * TILE, b * 128 : (b + 1) * 128]
                    full = full + jnp.concatenate([low] * b + [tap] + [low] * (2 - b), axis=0)
                full = jnp.where(active[j], full, 0.0)
                gathered = gathered + full
                row_acc[pl.ds(p, 1), :] = jnp.sum(full, axis=0, keepdims=True)
            col_acc[...] += gathered

        @pl.when(col_start < total_bins)
        def _():
            pl.loop(0, ext // STEP)(lambda k: sweep(k, 3))

        @pl.when(col_start >= total_bins)
        def _():
            pl.loop(0, ext // STEP)(lambda k: sweep(k, 1))

        feat_acc[pl.ds(row_start, ext), :] += row_acc[...]
        feat_acc[pl.ds(col_start, wide), :] += col_acc[...]
        for p in range(0, sub_rows, 16):
            block = preds[2 * RATE + p : 2 * RATE + p + 16]
            pred_ref[0, :, p : p + 16, :] = jnp.transpose(block, (1, 0, 2)).astype(jnp.bfloat16)

    @pl.when(slot == pl.num_programs(0) - 1)
    def _():
        flat[...] = jnp.zeros_like(flat)
        for a in range(3):
            for b in range(3):
                at = (a * 3 + b) * out_channels
                flat[at : at + out_channels, :] = weight_acc[
                    a * out_channels : (a + 1) * out_channels, b * 128 : (b + 1) * 128
                ]
        flat[3 * stacked : 3 * stacked + out_channels, :] = bias_acc[...]

        @pl.loop(0, tiles)
        def _(t):
            for half in range(2):
                start = pl.multiple_of(RATE + (t * 2 + half) * feat_rows, RATE)
                part_ref[half, t, 0:feat_rows, :] = feat_acc[pl.ds(start, feat_rows), :]
                at = pl.multiple_of((half * tiles + t) * chunk_rows, RATE)
                part_ref[half, t, feat_rows:, :] = flat[pl.ds(at, chunk_rows), :]


def reduce_kernel(
    tiles, feat_rows, part_ref, feat_ref, out_ref,
    from_core, comb, from_tiles, sending, own_feat, gathered,
    core_sem, scatter_sem, gather_sem, forward_sem, feat_sem, load_sem,
):
    me = lax.axis_index("tile")
    sub = lax.axis_index("sub")
    other = 1 - sub

    def peer_of(d):
        return lax.rem(me + d, tiles)

    def source_of(d):
        return lax.rem(me - d + tiles, tiles)

    def remote(src, dst, sems, where):
        return pltpu.make_async_remote_copy(
            src_ref=src, dst_ref=dst, send_sem=sems[0], recv_sem=sems[1],
            device_id=where, device_id_type=MESH,
        )

    load = pltpu.make_async_copy(part_ref.at[sub], comb, load_sem)
    load.start()
    barrier = pltpu.get_barrier_semaphore()
    pl.semaphore_signal(barrier, inc=1, device_id={"sub": other}, device_id_type=MESH)

    def greet(d, carry):
        pl.semaphore_signal(barrier, inc=1, device_id={"tile": peer_of(d)}, device_id_type=MESH)
        return carry

    lax.fori_loop(1, tiles, greet, 0)
    pl.semaphore_wait(barrier, tiles)

    core = remote(
        part_ref.at[other], from_core, (core_sem.at[0], core_sem.at[1]), {"sub": other}
    )
    core.start()
    load.wait()
    core.wait()
    comb[...] += from_core[...]
    sending[...] = comb[...].astype(sending.dtype)

    def scatter_of(d):
        return remote(
            sending.at[peer_of(d)], from_tiles.at[d],
            (scatter_sem.at[0, d], scatter_sem.at[1, d]), {"tile": peer_of(d)},
        )

    def scatter_start(d, carry):
        scatter_of(d).start()
        return carry

    lax.fori_loop(1, tiles, scatter_start, 0)

    def scatter_add(d, total):
        scatter_of(d).wait()
        return total + from_tiles[d].astype(jnp.float32)

    total = lax.fori_loop(1, tiles, scatter_add, comb[me])
    own_feat[sub] = total[0:feat_rows]
    gathered[sub, me] = total[feat_rows:].astype(gathered.dtype)

    def gather_of(d):
        return remote(
            gathered.at[sub, me], gathered.at[sub, me],
            (gather_sem.at[0, d], gather_sem.at[1, d]), {"tile": peer_of(d)},
        )

    def forward_of(d):
        source = source_of(d)
        return remote(
            gathered.at[sub, source], gathered.at[sub, source],
            (forward_sem.at[0, d], forward_sem.at[1, d]), {"sub": other},
        )

    def gather_start(d, carry):
        gather_of(d).start()
        return carry

    lax.fori_loop(1, tiles, gather_start, 0)
    feat_copy = remote(
        own_feat.at[sub], own_feat.at[sub], (feat_sem.at[0], feat_sem.at[1]), {"sub": other}
    )
    feat_copy.start()
    forward_of(0).start()

    def forward(d, carry):
        gather_of(d).wait()
        forward_of(d).start()
        return carry

    lax.fori_loop(1, tiles, forward, 0)

    def forward_end(d, carry):
        forward_of(d).wait()
        return carry

    lax.fori_loop(0, tiles, forward_end, 0)
    feat_copy.wait()
    feat_ref[...] = own_feat[...]
    out_ref[...] = gathered[...]


def finish_kernel(weight_rows, feat_in, sums_in, feat_ref, weight_ref, bias_ref):
    feat_ref[...] = feat_in[...].reshape(feat_ref.shape)
    sums = sums_in[...].astype(jnp.float32).reshape(-1, feat_ref.shape[1])
    weight_ref[...] = sums[:weight_rows]
    bias = sums[weight_rows : weight_rows + bias_ref.shape[1]]
    bias_ref[...] = jnp.sum(jnp.transpose(bias, (1, 0)), axis=0, keepdims=True)


def on_device(tiles, subs, features, weight, out_bias, band_tiles, band_width, cotangent):
    rows, channels = features.shape
    slots, out_channels, sub_rows, _ = cotangent.shape
    total_bins = tiles * rows
    stacked = 3 * out_channels
    vmem = pl.BlockSpec(memory_space=pltpu.VMEM)
    padded = pl.pallas_call(
        functools.partial(gather_kernel, tiles),
        out_shape=jax.ShapeDtypeStruct((total_bins + TILE + 2 * RATE, channels), jnp.float32),
        in_specs=[vmem],
        out_specs=vmem,
        scratch_shapes=[
            pltpu.VMEM((tiles, rows, channels), features.dtype),
            pltpu.SemaphoreType.DMA((tiles,)),
            pltpu.SemaphoreType.DMA((tiles,)),
        ],
        compiler_params=pltpu.CompilerParams(
            collective_id=0, has_side_effects=True, vmem_limit_bytes=64 << 20
        ),
    )(features)

    feat_rows = rows // 2
    flat_rows = 3 * stacked + out_channels
    chunk_rows = -(-flat_rows // (2 * tiles * 16)) * 16
    part_rows = feat_rows + chunk_rows
    ext = sub_rows + 2 * RATE
    wide = TILE + 2 * RATE
    padded_rows = total_bins + wide

    def whole(shape):
        return pl.BlockSpec(shape, lambda i, *_: (0,) * len(shape))

    hbm = pl.BlockSpec(memory_space=pltpu.HBM)
    block = pl.BlockSpec((1, out_channels, sub_rows, TILE), lambda i, *_: (i, 0, 0, 0))
    prediction, part = pl.pallas_call(
        functools.partial(compute_kernel, sub_rows, tiles, chunk_rows, feat_rows, total_bins),
        out_shape=(
            jax.ShapeDtypeStruct(cotangent.shape, jnp.bfloat16),
            jax.ShapeDtypeStruct((2, tiles, part_rows, channels), jnp.float32),
        ),
        grid_spec=pltpu.PrefetchScalarGridSpec(
            num_scalar_prefetch=0,
            grid=(slots,),
            in_specs=[
                hbm,
                hbm,
                whole((padded_rows, channels)),
                whole(weight.shape),
                whole((1, out_channels)),
                hbm,
            ],
            out_specs=[block, whole((2, tiles, part_rows, channels))],
            scratch_shapes=[
                pltpu.SMEM(band_tiles.shape, jnp.int32),
                pltpu.SMEM(band_width.shape, jnp.int32),
                pltpu.VMEM(cotangent.shape, cotangent.dtype),
                pltpu.VMEM((stacked, 3 * channels), weight.dtype),
                pltpu.VMEM((out_channels, TILE), jnp.float32),
                pltpu.VMEM((sub_rows + 4 * RATE, out_channels, TILE), jnp.bfloat16),
                pltpu.VMEM((sub_rows + 4 * RATE, out_channels, TILE), jnp.float32),
                pltpu.VMEM((wide, channels), jnp.float32),
                pltpu.VMEM((ext, channels), jnp.float32),
                pltpu.VMEM((stacked, 3 * channels), jnp.float32),
                pltpu.VMEM((out_channels, TILE), jnp.float32),
                pltpu.VMEM((padded_rows, channels), jnp.float32),
                pltpu.VMEM((2 * tiles * chunk_rows, channels), jnp.float32),
                pltpu.SemaphoreType.DMA((2,)),
                pltpu.SemaphoreType.DMA((slots,)),
            ],
        ),
        compiler_params=pltpu.CompilerParams(vmem_limit_bytes=64 << 20),
    )(band_tiles, band_width, padded, weight, out_bias.reshape(1, out_channels), cotangent)

    feature_grad, sums = pl.pallas_call(
        functools.partial(reduce_kernel, tiles, feat_rows),
        out_shape=(
            jax.ShapeDtypeStruct((2, feat_rows, channels), jnp.float32),
            jax.ShapeDtypeStruct((2, tiles, chunk_rows, channels), jnp.bfloat16),
        ),
        in_specs=[hbm],
        out_specs=(vmem, vmem),
        scratch_shapes=[
            pltpu.VMEM((tiles, part_rows, channels), jnp.float32),
            pltpu.VMEM((tiles, part_rows, channels), jnp.float32),
            pltpu.VMEM((tiles, part_rows, channels), jnp.bfloat16),
            pltpu.VMEM((tiles, part_rows, channels), jnp.bfloat16),
            pltpu.VMEM((2, feat_rows, channels), jnp.float32),
            pltpu.VMEM((2, tiles, chunk_rows, channels), jnp.bfloat16),
            pltpu.SemaphoreType.DMA((2,)),
            pltpu.SemaphoreType.DMA((2, tiles)),
            pltpu.SemaphoreType.DMA((2, tiles)),
            pltpu.SemaphoreType.DMA((2, tiles)),
            pltpu.SemaphoreType.DMA((2,)),
            pltpu.SemaphoreType.DMA,
        ],
        compiler_params=pltpu.CompilerParams(
            collective_id=1, has_side_effects=True, vmem_limit_bytes=(64 << 20) - (380 << 10)
        ),
    )(part)
    feature_grad, weight_grad, bias_grad = pl.pallas_call(
        functools.partial(finish_kernel, 3 * stacked),
        out_shape=(
            jax.ShapeDtypeStruct((rows, channels), jnp.float32),
            jax.ShapeDtypeStruct((3 * stacked, channels), jnp.float32),
            jax.ShapeDtypeStruct((1, out_channels), jnp.float32),
        ),
        in_specs=[vmem, vmem],
        out_specs=(vmem, vmem, vmem),
        compiler_params=pltpu.CompilerParams(vmem_limit_bytes=64 << 20),
    )(feature_grad, sums)
    return (
        prediction,
        feature_grad,
        weight_grad.reshape(weight.shape),
        bias_grad.reshape(out_channels),
    )


def solution(mesh):
    in_specs = (
        P(("groups", "tile"), None),
        P(),
        P(),
        P(("groups", "tile")),
        P("groups"),
        P(("groups", "tile"), None, "sub", None),
    )
    out_specs = (
        P(("groups", "tile"), None, "sub", None),
        P(("groups", "tile"), None),
        P("groups", None, None, None),
        P("groups"),
    )
    return jax.shard_map(
        functools.partial(on_device, mesh.shape["tile"], mesh.shape["sub"]),
        mesh=mesh, in_specs=in_specs, out_specs=out_specs, check_vma=False,
    )
```

```python
import functools

import jax
import jax.numpy as jnp
from jax import lax
from jax.experimental import pallas as pl
from jax.experimental.pallas import tpu as pltpu
from jax.sharding import PartitionSpec as P

RATE = 8
TILE = 128
BAND_T = 8
FAR = -1e30
STEP = 40
MESH = pl.DeviceIdType.MESH


def gather_kernel(tiles, x_ref, out_ref, held, send_sem, recv_sem):
    me = lax.axis_index("tile")
    rows = x_ref.shape[0]
    total = tiles * rows

    def peer_of(d):
        return lax.rem(me + d, tiles)

    barrier = pltpu.get_barrier_semaphore()

    def greet(d, carry):
        pl.semaphore_signal(barrier, inc=1, device_id={"tile": peer_of(d)}, device_id_type=MESH)
        return carry

    lax.fori_loop(1, tiles, greet, 0)
    pl.semaphore_wait(barrier, tiles - 1)

    def copy_of(d):
        return pltpu.make_async_remote_copy(
            src_ref=x_ref,
            dst_ref=held.at[me],
            send_sem=send_sem.at[d],
            recv_sem=recv_sem.at[d],
            device_id={"tile": peer_of(d)},
            device_id_type=MESH,
        )

    def start(d, carry):
        copy_of(d).start()
        return carry

    lax.fori_loop(1, tiles, start, 0)
    out_ref[0:RATE, :] = jnp.full((RATE, 128), FAR, jnp.float32)
    tail = out_ref.shape[0] - RATE - total
    out_ref[RATE + total :, :] = jnp.full((tail, 128), FAR, jnp.float32)
    own = pl.multiple_of(RATE + me * rows, RATE)
    out_ref[pl.ds(own, rows), :] = x_ref[...].astype(jnp.float32)

    def finish(d, carry):
        copy_of(d).wait()
        source = lax.rem(me - d + tiles, tiles)
        at = pl.multiple_of(RATE + source * rows, RATE)
        out_ref[pl.ds(at, rows), :] = held[source].astype(jnp.float32)
        return carry

    lax.fori_loop(1, tiles, finish, 0)


def compute_kernel(
    sub_rows, tiles, chunk_rows, feat_rows, total_bins,
    ids_hbm, width_hbm, feat_ref, weight_in, bias_in, cot_hbm,
    pred_ref, part_ref,
    ids_ref, width_ref, cots, weight_ref, bias_ref,
    grads, preds, col_acc, row_acc, weight_acc, bias_acc, feat_acc, flat,
    table_sem, cot_sem,
):
    slot = pl.program_id(0)
    slots, out_channels = cots.shape[:2]
    cot_ref = cots.at[pl.ds(slot, 1)]
    sub = lax.axis_index("sub")

    def cot_copy(at):
        return pltpu.make_async_copy(cot_hbm.at[at], cots.at[at], cot_sem.at[at])

    stacked = 3 * out_channels
    ext = sub_rows + 2 * RATE
    wide = TILE + 2 * RATE

    @pl.when(slot == 0)
    def _():
        ids_copy = pltpu.make_async_copy(ids_hbm, ids_ref, table_sem.at[0])
        width_copy = pltpu.make_async_copy(width_hbm, width_ref, table_sem.at[1])
        ids_copy.start()
        width_copy.start()
        for at in range(slots):
            cot_copy(at).start()
        for a in range(3):
            for b in range(3):
                weight_ref[
                    a * out_channels : (a + 1) * out_channels, b * 128 : (b + 1) * 128
                ] = weight_in[a, b]
        bias_ref[...] = jnp.transpose(
            jnp.broadcast_to(bias_in[...], (TILE, out_channels)), (1, 0)
        )
        weight_acc[...] = jnp.zeros_like(weight_acc)
        bias_acc[...] = jnp.zeros_like(bias_acc)
        feat_acc[...] = jnp.zeros_like(feat_acc)
        pad = jnp.zeros((2 * RATE, out_channels, TILE), grads.dtype)
        grads[0 : 2 * RATE] = pad
        grads[2 * RATE + sub_rows : 4 * RATE + sub_rows] = pad
        ids_copy.wait()
        width_copy.wait()

    cot_copy(slot).wait()

    tile_id = ids_ref[slot]
    tile_row = tile_id // BAND_T
    offset = tile_id - tile_row * BAND_T
    valid = offset < width_ref[tile_row]
    row_start = pl.multiple_of(tile_row * TILE + sub * sub_rows, RATE)
    col_start = pl.multiple_of((tile_row + offset) * TILE, TILE)
    reaches = jnp.logical_and(valid, col_start <= total_bins)

    @pl.when(jnp.logical_not(valid))
    def _():
        pred_ref[...] = jnp.zeros_like(pred_ref)

    @pl.when(valid)
    def _():
        total = jnp.zeros((out_channels, 16, TILE), jnp.float32)
        for p in range(0, sub_rows, 16):
            total = total + cot_ref[0, :, p : p + 16, :].astype(jnp.float32)
        bias_acc[...] += jnp.sum(total, axis=1)

    @pl.when(jnp.logical_and(valid, jnp.logical_not(reaches)))
    def _():
        filled = jnp.broadcast_to(bias_ref[...][:, None, :], (out_channels, 16, TILE))
        filled = filled.astype(jnp.bfloat16)
        for p in range(0, sub_rows, 16):
            pred_ref[0, :, p : p + 16, :] = filled

    @pl.when(reaches)
    def _():
        for p in range(0, sub_rows, 16):
            block = cot_ref[0, :, p : p + 16, :].astype(jnp.float32)
            grads[2 * RATE + p : 2 * RATE + p + 16] = jnp.transpose(block, (1, 0, 2)).astype(
                grads.dtype
            )
        bias_rows = bias_ref[...]

        @pl.loop(0, sub_rows + 4 * RATE)
        def _(p):
            preds[p] = bias_rows

        col_acc[...] = jnp.zeros_like(col_acc)

        def sweep(k, columns):
            first = k * STEP
            taps_wide = columns * 128
            col_feat = feat_ref[pl.ds(col_start, wide), :]
            hidden, active, stacks = [], [], []
            for j in range(STEP):
                p = first + j
                pair = feat_ref[pl.ds(row_start + p, 1), :] + col_feat
                active.append(pair > 0.0)
                relu = jnp.maximum(pair, 0.0)
                hidden.append(
                    jnp.concatenate(
                        [relu[RATE * b : RATE * b + TILE].astype(jnp.bfloat16) for b in range(columns)],
                        axis=1,
                    )
                )
                stacks.append(
                    jnp.concatenate([grads[p + RATE * (2 - a)] for a in range(3)], axis=0)
                )
            hidden_all = jnp.concatenate(hidden, axis=0)
            stack_all = jnp.concatenate(stacks, axis=1)
            weights = weight_ref[:, 0:taps_wide]
            weight_acc[:, 0:taps_wide] += jnp.dot(
                stack_all, hidden_all, preferred_element_type=jnp.float32
            )
            shifted = lax.dot_general(
                weights, hidden_all, (((1,), (1,)), ((), ())),
                preferred_element_type=jnp.float32,
            )
            back = lax.dot_general(
                stack_all, weights, (((0,), (0,)), ((), ())),
                preferred_element_type=jnp.float32,
            )
            gathered = jnp.zeros((wide, TILE), jnp.float32)
            low = jnp.zeros((RATE, TILE), jnp.float32)
            for j in range(STEP):
                p = first + j
                for a in range(3):
                    preds[p + RATE * (2 - a)] += shifted[
                        a * out_channels : (a + 1) * out_channels, j * TILE : (j + 1) * TILE
                    ]
                full = jnp.zeros((wide, TILE), jnp.float32)
                for b in range(columns):
                    tap = back[j * TILE : (j + 1) * TILE, b * 128 : (b + 1) * 128]
                    full = full + jnp.concatenate([low] * b + [tap] + [low] * (2 - b), axis=0)
                full = jnp.where(active[j], full, 0.0)
                gathered = gathered + full
                row_acc[pl.ds(p, 1), :] = jnp.sum(full, axis=0, keepdims=True)
            col_acc[...] += gathered

        @pl.when(col_start < total_bins)
        def _():
            pl.loop(0, ext // STEP)(lambda k: sweep(k, 3))

        @pl.when(col_start >= total_bins)
        def _():
            pl.loop(0, ext // STEP)(lambda k: sweep(k, 1))

        feat_acc[pl.ds(row_start, ext), :] += row_acc[...]
        feat_acc[pl.ds(col_start, wide), :] += col_acc[...]
        for p in range(0, sub_rows, 16):
            block = preds[2 * RATE + p : 2 * RATE + p + 16]
            pred_ref[0, :, p : p + 16, :] = jnp.transpose(block, (1, 0, 2)).astype(jnp.bfloat16)

    @pl.when(slot == pl.num_programs(0) - 1)
    def _():
        flat[...] = jnp.zeros_like(flat)
        for a in range(3):
            for b in range(3):
                at = (a * 3 + b) * out_channels
                flat[at : at + out_channels, :] = weight_acc[
                    a * out_channels : (a + 1) * out_channels, b * 128 : (b + 1) * 128
                ]
        flat[3 * stacked : 3 * stacked + out_channels, :] = bias_acc[...]

        @pl.loop(0, tiles)
        def _(t):
            for half in range(2):
                start = pl.multiple_of(RATE + (t * 2 + half) * feat_rows, RATE)
                part_ref[half, t, 0:feat_rows, :] = feat_acc[pl.ds(start, feat_rows), :]
                at = pl.multiple_of((half * tiles + t) * chunk_rows, RATE)
                part_ref[half, t, feat_rows:, :] = flat[pl.ds(at, chunk_rows), :]


def reduce_kernel(
    tiles, feat_rows, part_ref, feat_ref, out_ref,
    from_core, comb, from_tiles, sending, own_feat, gathered,
    core_sem, scatter_sem, gather_sem, forward_sem, feat_sem, load_sem,
):
    me = lax.axis_index("tile")
    sub = lax.axis_index("sub")
    other = 1 - sub

    def peer_of(d):
        return lax.rem(me + d, tiles)

    def source_of(d):
        return lax.rem(me - d + tiles, tiles)

    def remote(src, dst, sems, where):
        return pltpu.make_async_remote_copy(
            src_ref=src, dst_ref=dst, send_sem=sems[0], recv_sem=sems[1],
            device_id=where, device_id_type=MESH,
        )

    load = pltpu.make_async_copy(part_ref.at[sub], comb, load_sem)
    load.start()
    barrier = pltpu.get_barrier_semaphore()
    pl.semaphore_signal(barrier, inc=1, device_id={"sub": other}, device_id_type=MESH)

    def greet(d, carry):
        pl.semaphore_signal(barrier, inc=1, device_id={"tile": peer_of(d)}, device_id_type=MESH)
        return carry

    lax.fori_loop(1, tiles, greet, 0)
    pl.semaphore_wait(barrier, tiles)

    core = remote(
        part_ref.at[other], from_core, (core_sem.at[0], core_sem.at[1]), {"sub": other}
    )
    core.start()
    load.wait()
    core.wait()
    comb[...] += from_core[...]
    sending[...] = comb[...].astype(sending.dtype)

    def scatter_of(d):
        return remote(
            sending.at[peer_of(d)], from_tiles.at[d],
            (scatter_sem.at[0, d], scatter_sem.at[1, d]), {"tile": peer_of(d)},
        )

    def scatter_start(d, carry):
        scatter_of(d).start()
        return carry

    lax.fori_loop(1, tiles, scatter_start, 0)

    def scatter_add(d, total):
        scatter_of(d).wait()
        return total + from_tiles[d].astype(jnp.float32)

    total = lax.fori_loop(1, tiles, scatter_add, comb[me])
    own_feat[sub] = total[0:feat_rows]
    gathered[sub, me] = total[feat_rows:].astype(gathered.dtype)

    def gather_of(d):
        return remote(
            gathered.at[sub, me], gathered.at[sub, me],
            (gather_sem.at[0, d], gather_sem.at[1, d]), {"tile": peer_of(d)},
        )

    def forward_of(d):
        source = source_of(d)
        return remote(
            gathered.at[sub, source], gathered.at[sub, source],
            (forward_sem.at[0, d], forward_sem.at[1, d]), {"sub": other},
        )

    def gather_start(d, carry):
        gather_of(d).start()
        return carry

    lax.fori_loop(1, tiles, gather_start, 0)
    feat_copy = remote(
        own_feat.at[sub], own_feat.at[sub], (feat_sem.at[0], feat_sem.at[1]), {"sub": other}
    )
    feat_copy.start()
    forward_of(0).start()

    def forward(d, carry):
        gather_of(d).wait()
        forward_of(d).start()
        return carry

    lax.fori_loop(1, tiles, forward, 0)

    def forward_end(d, carry):
        forward_of(d).wait()
        return carry

    lax.fori_loop(0, tiles, forward_end, 0)
    feat_copy.wait()
    feat_ref[...] = own_feat[...]
    out_ref[...] = gathered[...]


def finish_kernel(weight_rows, feat_in, sums_in, feat_ref, weight_ref, bias_ref):
    feat_ref[...] = feat_in[...].reshape(feat_ref.shape)
    sums = sums_in[...].astype(jnp.float32).reshape(-1, feat_ref.shape[1])
    weight_ref[...] = sums[:weight_rows]
    bias = sums[weight_rows : weight_rows + bias_ref.shape[1]]
    bias_ref[...] = jnp.sum(jnp.transpose(bias, (1, 0)), axis=0, keepdims=True)


def on_device(tiles, subs, features, weight, out_bias, band_tiles, band_width, cotangent):
    rows, channels = features.shape
    slots, out_channels, sub_rows, _ = cotangent.shape
    total_bins = tiles * rows
    stacked = 3 * out_channels
    vmem = pl.BlockSpec(memory_space=pltpu.VMEM)
    padded = pl.pallas_call(
        functools.partial(gather_kernel, tiles),
        out_shape=jax.ShapeDtypeStruct((total_bins + TILE + 2 * RATE, channels), jnp.float32),
        in_specs=[vmem],
        out_specs=vmem,
        scratch_shapes=[
            pltpu.VMEM((tiles, rows, channels), features.dtype),
            pltpu.SemaphoreType.DMA((tiles,)),
            pltpu.SemaphoreType.DMA((tiles,)),
        ],
        compiler_params=pltpu.CompilerParams(
            collective_id=0, has_side_effects=True, vmem_limit_bytes=64 << 20
        ),
    )(features)

    feat_rows = rows // 2
    flat_rows = 3 * stacked + out_channels
    chunk_rows = -(-flat_rows // (2 * tiles * 16)) * 16
    part_rows = feat_rows + chunk_rows
    ext = sub_rows + 2 * RATE
    wide = TILE + 2 * RATE
    padded_rows = total_bins + wide

    def whole(shape):
        return pl.BlockSpec(shape, lambda i, *_: (0,) * len(shape))

    hbm = pl.BlockSpec(memory_space=pltpu.HBM)
    block = pl.BlockSpec((1, out_channels, sub_rows, TILE), lambda i, *_: (i, 0, 0, 0))
    prediction, part = pl.pallas_call(
        functools.partial(compute_kernel, sub_rows, tiles, chunk_rows, feat_rows, total_bins),
        out_shape=(
            jax.ShapeDtypeStruct(cotangent.shape, jnp.bfloat16),
            jax.ShapeDtypeStruct((2, tiles, part_rows, channels), jnp.float32),
        ),
        grid_spec=pltpu.PrefetchScalarGridSpec(
            num_scalar_prefetch=0,
            grid=(slots,),
            in_specs=[
                hbm,
                hbm,
                whole((padded_rows, channels)),
                whole(weight.shape),
                whole((1, out_channels)),
                hbm,
            ],
            out_specs=[block, whole((2, tiles, part_rows, channels))],
            scratch_shapes=[
                pltpu.SMEM(band_tiles.shape, jnp.int32),
                pltpu.SMEM(band_width.shape, jnp.int32),
                pltpu.VMEM(cotangent.shape, cotangent.dtype),
                pltpu.VMEM((stacked, 3 * channels), weight.dtype),
                pltpu.VMEM((out_channels, TILE), jnp.float32),
                pltpu.VMEM((sub_rows + 4 * RATE, out_channels, TILE), jnp.bfloat16),
                pltpu.VMEM((sub_rows + 4 * RATE, out_channels, TILE), jnp.float32),
                pltpu.VMEM((wide, channels), jnp.float32),
                pltpu.VMEM((ext, channels), jnp.float32),
                pltpu.VMEM((stacked, 3 * channels), jnp.float32),
                pltpu.VMEM((out_channels, TILE), jnp.float32),
                pltpu.VMEM((padded_rows, channels), jnp.float32),
                pltpu.VMEM((2 * tiles * chunk_rows, channels), jnp.float32),
                pltpu.SemaphoreType.DMA((2,)),
                pltpu.SemaphoreType.DMA((slots,)),
            ],
        ),
        compiler_params=pltpu.CompilerParams(vmem_limit_bytes=64 << 20),
    )(band_tiles, band_width, padded, weight, out_bias.reshape(1, out_channels), cotangent)

    feature_grad, sums = pl.pallas_call(
        functools.partial(reduce_kernel, tiles, feat_rows),
        out_shape=(
            jax.ShapeDtypeStruct((2, feat_rows, channels), jnp.float32),
            jax.ShapeDtypeStruct((2, tiles, chunk_rows, channels), jnp.bfloat16),
        ),
        in_specs=[hbm],
        out_specs=(vmem, vmem),
        scratch_shapes=[
            pltpu.VMEM((tiles, part_rows, channels), jnp.float32),
            pltpu.VMEM((tiles, part_rows, channels), jnp.float32),
            pltpu.VMEM((tiles, part_rows, channels), jnp.bfloat16),
            pltpu.VMEM((tiles, part_rows, channels), jnp.bfloat16),
            pltpu.VMEM((2, feat_rows, channels), jnp.float32),
            pltpu.VMEM((2, tiles, chunk_rows, channels), jnp.bfloat16),
            pltpu.SemaphoreType.DMA((2,)),
            pltpu.SemaphoreType.DMA((2, tiles)),
            pltpu.SemaphoreType.DMA((2, tiles)),
            pltpu.SemaphoreType.DMA((2, tiles)),
            pltpu.SemaphoreType.DMA((2,)),
            pltpu.SemaphoreType.DMA,
        ],
        compiler_params=pltpu.CompilerParams(
            collective_id=1, has_side_effects=True, vmem_limit_bytes=(64 << 20) - (380 << 10)
        ),
    )(part)
    feature_grad, weight_grad, bias_grad = pl.pallas_call(
        functools.partial(finish_kernel, 3 * stacked),
        out_shape=(
            jax.ShapeDtypeStruct((rows, channels), jnp.float32),
            jax.ShapeDtypeStruct((3 * stacked, channels), jnp.float32),
            jax.ShapeDtypeStruct((1, out_channels), jnp.float32),
        ),
        in_specs=[vmem, vmem],
        out_specs=(vmem, vmem, vmem),
        compiler_params=pltpu.CompilerParams(vmem_limit_bytes=64 << 20),
    )(feature_grad, sums)
    return (
        prediction,
        feature_grad,
        weight_grad.reshape(weight.shape),
        bias_grad.reshape(out_channels),
    )


def solution(mesh):
    in_specs = (
        P(("groups", "tile"), None),
        P(),
        P(),
        P(("groups", "tile")),
        P("groups"),
        P(("groups", "tile"), None, "sub", None),
    )
    out_specs = (
        P(("groups", "tile"), None, "sub", None),
        P(("groups", "tile"), None),
        P("groups", None, None, None),
        P("groups"),
    )
    return jax.shard_map(
        functools.partial(on_device, mesh.shape["tile"], mesh.shape["sub"]),
        mesh=mesh, in_specs=in_specs, out_specs=out_specs, check_vma=False,
    )
```

```python
import functools

import jax
import jax.numpy as jnp
from jax import lax
from jax.experimental import pallas as pl
from jax.experimental.pallas import tpu as pltpu
from jax.sharding import PartitionSpec as P

RATE = 8
TILE = 128
BAND_T = 8
FAR = -1e30
STEP = 40
MESH = pl.DeviceIdType.MESH


def gather_kernel(tiles, x_ref, out_ref, held, send_sem, recv_sem):
    me = lax.axis_index("tile")
    rows = x_ref.shape[0]
    total = tiles * rows

    def peer_of(d):
        return lax.rem(me + d, tiles)

    barrier = pltpu.get_barrier_semaphore()

    def greet(d, carry):
        pl.semaphore_signal(barrier, inc=1, device_id={"tile": peer_of(d)}, device_id_type=MESH)
        return carry

    lax.fori_loop(1, tiles, greet, 0)
    pl.semaphore_wait(barrier, tiles - 1)

    def copy_of(d):
        return pltpu.make_async_remote_copy(
            src_ref=x_ref,
            dst_ref=held.at[me],
            send_sem=send_sem.at[d],
            recv_sem=recv_sem.at[d],
            device_id={"tile": peer_of(d)},
            device_id_type=MESH,
        )

    def start(d, carry):
        copy_of(d).start()
        return carry

    lax.fori_loop(1, tiles, start, 0)
    out_ref[0:RATE, :] = jnp.full((RATE, 128), FAR, jnp.float32)
    tail = out_ref.shape[0] - RATE - total
    out_ref[RATE + total :, :] = jnp.full((tail, 128), FAR, jnp.float32)
    own = pl.multiple_of(RATE + me * rows, RATE)
    out_ref[pl.ds(own, rows), :] = x_ref[...].astype(jnp.float32)

    def finish(d, carry):
        copy_of(d).wait()
        source = lax.rem(me - d + tiles, tiles)
        at = pl.multiple_of(RATE + source * rows, RATE)
        out_ref[pl.ds(at, rows), :] = held[source].astype(jnp.float32)
        return carry

    lax.fori_loop(1, tiles, finish, 0)


def compute_kernel(
    sub_rows, tiles, chunk_rows, feat_rows, total_bins,
    ids_hbm, width_hbm, feat_ref, weight_in, bias_in, cot_hbm,
    pred_ref, part_ref,
    ids_ref, width_ref, cots, weight_ref, bias_ref,
    grads, preds, col_acc, row_acc, weight_acc, bias_acc, feat_acc, flat,
    table_sem, cot_sem,
):
    slot = pl.program_id(0)
    slots, out_channels = cots.shape[:2]
    cot_ref = cots.at[pl.ds(slot, 1)]
    sub = lax.axis_index("sub")

    def cot_copy(at):
        return pltpu.make_async_copy(cot_hbm.at[at], cots.at[at], cot_sem.at[at])

    stacked = 3 * out_channels
    ext = sub_rows + 2 * RATE
    wide = TILE + 2 * RATE

    @pl.when(slot == 0)
    def _():
        ids_copy = pltpu.make_async_copy(ids_hbm, ids_ref, table_sem.at[0])
        width_copy = pltpu.make_async_copy(width_hbm, width_ref, table_sem.at[1])
        ids_copy.start()
        width_copy.start()
        for at in range(slots):
            cot_copy(at).start()
        for a in range(3):
            for b in range(3):
                weight_ref[
                    a * out_channels : (a + 1) * out_channels, b * 128 : (b + 1) * 128
                ] = weight_in[a, b]
        bias_ref[...] = jnp.transpose(
            jnp.broadcast_to(bias_in[...], (TILE, out_channels)), (1, 0)
        )
        weight_acc[...] = jnp.zeros_like(weight_acc)
        bias_acc[...] = jnp.zeros_like(bias_acc)
        feat_acc[...] = jnp.zeros_like(feat_acc)
        pad = jnp.zeros((2 * RATE, out_channels, TILE), grads.dtype)
        grads[0 : 2 * RATE] = pad
        grads[2 * RATE + sub_rows : 4 * RATE + sub_rows] = pad
        ids_copy.wait()
        width_copy.wait()

    cot_copy(slot).wait()

    tile_id = ids_ref[slot]
    tile_row = tile_id // BAND_T
    offset = tile_id - tile_row * BAND_T
    valid = offset < width_ref[tile_row]
    row_start = pl.multiple_of(tile_row * TILE + sub * sub_rows, RATE)
    col_start = pl.multiple_of((tile_row + offset) * TILE, TILE)
    reaches = jnp.logical_and(valid, col_start <= total_bins)

    @pl.when(jnp.logical_not(valid))
    def _():
        pred_ref[...] = jnp.zeros_like(pred_ref)

    @pl.when(valid)
    def _():
        total = jnp.zeros((out_channels, 16, TILE), jnp.float32)
        for p in range(0, sub_rows, 16):
            total = total + cot_ref[0, :, p : p + 16, :].astype(jnp.float32)
        bias_acc[...] += jnp.sum(total, axis=1)

    @pl.when(jnp.logical_and(valid, jnp.logical_not(reaches)))
    def _():
        filled = jnp.broadcast_to(bias_ref[...][:, None, :], (out_channels, 16, TILE))
        filled = filled.astype(jnp.bfloat16)
        for p in range(0, sub_rows, 16):
            pred_ref[0, :, p : p + 16, :] = filled

    @pl.when(reaches)
    def _():
        for p in range(0, sub_rows, 16):
            block = cot_ref[0, :, p : p + 16, :].astype(jnp.float32)
            grads[2 * RATE + p : 2 * RATE + p + 16] = jnp.transpose(block, (1, 0, 2)).astype(
                grads.dtype
            )
        bias_rows = bias_ref[...]

        @pl.loop(0, sub_rows + 4 * RATE)
        def _(p):
            preds[p] = bias_rows

        col_acc[...] = jnp.zeros_like(col_acc)

        def sweep(k, columns):
            first = k * STEP
            taps_wide = columns * 128
            col_feat = feat_ref[pl.ds(col_start, wide), :]
            hidden, active, stacks = [], [], []
            for j in range(STEP):
                p = first + j
                pair = feat_ref[pl.ds(row_start + p, 1), :] + col_feat
                active.append(pair > 0.0)
                relu = jnp.maximum(pair, 0.0)
                hidden.append(
                    jnp.concatenate(
                        [relu[RATE * b : RATE * b + TILE].astype(jnp.bfloat16) for b in range(columns)],
                        axis=1,
                    )
                )
                stacks.append(
                    jnp.concatenate([grads[p + RATE * (2 - a)] for a in range(3)], axis=0)
                )
            hidden_all = jnp.concatenate(hidden, axis=0)
            stack_all = jnp.concatenate(stacks, axis=1)
            weights = weight_ref[:, 0:taps_wide]
            weight_acc[:, 0:taps_wide] += jnp.dot(
                stack_all, hidden_all, preferred_element_type=jnp.float32
            )
            shifted = lax.dot_general(
                weights, hidden_all, (((1,), (1,)), ((), ())),
                preferred_element_type=jnp.float32,
            )
            back = lax.dot_general(
                stack_all, weights, (((0,), (0,)), ((), ())),
                preferred_element_type=jnp.float32,
            )
            gathered = jnp.zeros((wide, TILE), jnp.float32)
            low = jnp.zeros((RATE, TILE), jnp.float32)
            for j in range(STEP):
                p = first + j
                for a in range(3):
                    preds[p + RATE * (2 - a)] += shifted[
                        a * out_channels : (a + 1) * out_channels, j * TILE : (j + 1) * TILE
                    ]
                full = jnp.zeros((wide, TILE), jnp.float32)
                for b in range(columns):
                    tap = back[j * TILE : (j + 1) * TILE, b * 128 : (b + 1) * 128]
                    full = full + jnp.concatenate([low] * b + [tap] + [low] * (2 - b), axis=0)
                full = jnp.where(active[j], full, 0.0)
                gathered = gathered + full
                row_acc[pl.ds(p, 1), :] = jnp.sum(full, axis=0, keepdims=True)
            col_acc[...] += gathered

        @pl.when(col_start < total_bins)
        def _():
            pl.loop(0, ext // STEP)(lambda k: sweep(k, 3))

        @pl.when(col_start >= total_bins)
        def _():
            pl.loop(0, ext // STEP)(lambda k: sweep(k, 1))

        feat_acc[pl.ds(row_start, ext), :] += row_acc[...]
        feat_acc[pl.ds(col_start, wide), :] += col_acc[...]
        for p in range(0, sub_rows, 16):
            block = preds[2 * RATE + p : 2 * RATE + p + 16]
            pred_ref[0, :, p : p + 16, :] = jnp.transpose(block, (1, 0, 2)).astype(jnp.bfloat16)

    @pl.when(slot == pl.num_programs(0) - 1)
    def _():
        flat[...] = jnp.zeros_like(flat)
        for a in range(3):
            for b in range(3):
                at = (a * 3 + b) * out_channels
                flat[at : at + out_channels, :] = weight_acc[
                    a * out_channels : (a + 1) * out_channels, b * 128 : (b + 1) * 128
                ]
        flat[3 * stacked : 3 * stacked + out_channels, :] = bias_acc[...]

        @pl.loop(0, tiles)
        def _(t):
            for half in range(2):
                start = pl.multiple_of(RATE + (t * 2 + half) * feat_rows, RATE)
                part_ref[half, t, 0:feat_rows, :] = feat_acc[pl.ds(start, feat_rows), :]
                at = pl.multiple_of((half * tiles + t) * chunk_rows, RATE)
                part_ref[half, t, feat_rows:, :] = flat[pl.ds(at, chunk_rows), :]


def reduce_kernel(
    tiles, feat_rows, part_ref, feat_ref, out_ref,
    from_core, comb, from_tiles, sending, own_feat, gathered,
    core_sem, scatter_sem, gather_sem, forward_sem, feat_sem, load_sem,
):
    me = lax.axis_index("tile")
    sub = lax.axis_index("sub")
    other = 1 - sub

    def peer_of(d):
        return lax.rem(me + d, tiles)

    def source_of(d):
        return lax.rem(me - d + tiles, tiles)

    def near_first(i):
        odd = lax.rem(i, 2)
        return odd * ((i + 1) // 2) + (1 - odd) * (tiles - i // 2)

    def remote(src, dst, sems, where):
        return pltpu.make_async_remote_copy(
            src_ref=src, dst_ref=dst, send_sem=sems[0], recv_sem=sems[1],
            device_id=where, device_id_type=MESH,
        )

    load = pltpu.make_async_copy(part_ref.at[sub], comb, load_sem)
    load.start()
    barrier = pltpu.get_barrier_semaphore()
    pl.semaphore_signal(barrier, inc=1, device_id={"sub": other}, device_id_type=MESH)

    def greet(d, carry):
        pl.semaphore_signal(barrier, inc=1, device_id={"tile": peer_of(d)}, device_id_type=MESH)
        return carry

    lax.fori_loop(1, tiles, greet, 0)
    pl.semaphore_wait(barrier, tiles)

    core = remote(
        part_ref.at[other], from_core, (core_sem.at[0], core_sem.at[1]), {"sub": other}
    )
    core.start()
    load.wait()
    core.wait()
    comb[...] += from_core[...]
    sending[...] = comb[...].astype(sending.dtype)

    def scatter_of(d):
        return remote(
            sending.at[peer_of(d)], from_tiles.at[d],
            (scatter_sem.at[0, d], scatter_sem.at[1, d]), {"tile": peer_of(d)},
        )

    def scatter_start(i, carry):
        scatter_of(near_first(tiles - i)).start()
        return carry

    lax.fori_loop(1, tiles, scatter_start, 0)

    def scatter_add(d, total):
        scatter_of(d).wait()
        return total + from_tiles[d].astype(jnp.float32)

    total = lax.fori_loop(1, tiles, scatter_add, comb[me])
    own_feat[sub] = total[0:feat_rows]
    gathered[sub, me] = total[feat_rows:].astype(gathered.dtype)

    def gather_of(d):
        return remote(
            gathered.at[sub, me], gathered.at[sub, me],
            (gather_sem.at[0, d], gather_sem.at[1, d]), {"tile": peer_of(d)},
        )

    def forward_of(d):
        source = source_of(d)
        return remote(
            gathered.at[sub, source], gathered.at[sub, source],
            (forward_sem.at[0, d], forward_sem.at[1, d]), {"sub": other},
        )

    def gather_start(i, carry):
        gather_of(near_first(tiles - i)).start()
        return carry

    lax.fori_loop(1, tiles, gather_start, 0)
    feat_copy = remote(
        own_feat.at[sub], own_feat.at[sub], (feat_sem.at[0], feat_sem.at[1]), {"sub": other}
    )
    feat_copy.start()
    forward_of(0).start()

    def forward(i, carry):
        d = near_first(i)
        gather_of(d).wait()
        forward_of(d).start()
        return carry

    lax.fori_loop(1, tiles, forward, 0)

    def forward_end(d, carry):
        forward_of(d).wait()
        return carry

    lax.fori_loop(0, tiles, forward_end, 0)
    feat_copy.wait()
    feat_ref[...] = own_feat[...]
    out_ref[...] = gathered[...]


def finish_kernel(weight_rows, feat_in, sums_in, feat_ref, weight_ref, bias_ref):
    feat_ref[...] = feat_in[...].reshape(feat_ref.shape)
    sums = sums_in[...].astype(jnp.float32).reshape(-1, feat_ref.shape[1])
    weight_ref[...] = sums[:weight_rows]
    bias = sums[weight_rows : weight_rows + bias_ref.shape[1]]
    bias_ref[...] = jnp.sum(jnp.transpose(bias, (1, 0)), axis=0, keepdims=True)


def on_device(tiles, subs, features, weight, out_bias, band_tiles, band_width, cotangent):
    rows, channels = features.shape
    slots, out_channels, sub_rows, _ = cotangent.shape
    total_bins = tiles * rows
    stacked = 3 * out_channels
    vmem = pl.BlockSpec(memory_space=pltpu.VMEM)
    padded = pl.pallas_call(
        functools.partial(gather_kernel, tiles),
        out_shape=jax.ShapeDtypeStruct((total_bins + TILE + 2 * RATE, channels), jnp.float32),
        in_specs=[vmem],
        out_specs=vmem,
        scratch_shapes=[
            pltpu.VMEM((tiles, rows, channels), features.dtype),
            pltpu.SemaphoreType.DMA((tiles,)),
            pltpu.SemaphoreType.DMA((tiles,)),
        ],
        compiler_params=pltpu.CompilerParams(
            collective_id=0, has_side_effects=True, vmem_limit_bytes=64 << 20
        ),
    )(features)

    feat_rows = rows // 2
    flat_rows = 3 * stacked + out_channels
    chunk_rows = -(-flat_rows // (2 * tiles * 16)) * 16
    part_rows = feat_rows + chunk_rows
    ext = sub_rows + 2 * RATE
    wide = TILE + 2 * RATE
    padded_rows = total_bins + wide

    def whole(shape):
        return pl.BlockSpec(shape, lambda i, *_: (0,) * len(shape))

    hbm = pl.BlockSpec(memory_space=pltpu.HBM)
    block = pl.BlockSpec((1, out_channels, sub_rows, TILE), lambda i, *_: (i, 0, 0, 0))
    prediction, part = pl.pallas_call(
        functools.partial(compute_kernel, sub_rows, tiles, chunk_rows, feat_rows, total_bins),
        out_shape=(
            jax.ShapeDtypeStruct(cotangent.shape, jnp.bfloat16),
            jax.ShapeDtypeStruct((2, tiles, part_rows, channels), jnp.float32),
        ),
        grid_spec=pltpu.PrefetchScalarGridSpec(
            num_scalar_prefetch=0,
            grid=(slots,),
            in_specs=[
                hbm,
                hbm,
                whole((padded_rows, channels)),
                whole(weight.shape),
                whole((1, out_channels)),
                hbm,
            ],
            out_specs=[block, whole((2, tiles, part_rows, channels))],
            scratch_shapes=[
                pltpu.SMEM(band_tiles.shape, jnp.int32),
                pltpu.SMEM(band_width.shape, jnp.int32),
                pltpu.VMEM(cotangent.shape, cotangent.dtype),
                pltpu.VMEM((stacked, 3 * channels), weight.dtype),
                pltpu.VMEM((out_channels, TILE), jnp.float32),
                pltpu.VMEM((sub_rows + 4 * RATE, out_channels, TILE), jnp.bfloat16),
                pltpu.VMEM((sub_rows + 4 * RATE, out_channels, TILE), jnp.float32),
                pltpu.VMEM((wide, channels), jnp.float32),
                pltpu.VMEM((ext, channels), jnp.float32),
                pltpu.VMEM((stacked, 3 * channels), jnp.float32),
                pltpu.VMEM((out_channels, TILE), jnp.float32),
                pltpu.VMEM((padded_rows, channels), jnp.float32),
                pltpu.VMEM((2 * tiles * chunk_rows, channels), jnp.float32),
                pltpu.SemaphoreType.DMA((2,)),
                pltpu.SemaphoreType.DMA((slots,)),
            ],
        ),
        compiler_params=pltpu.CompilerParams(vmem_limit_bytes=64 << 20),
    )(band_tiles, band_width, padded, weight, out_bias.reshape(1, out_channels), cotangent)

    feature_grad, sums = pl.pallas_call(
        functools.partial(reduce_kernel, tiles, feat_rows),
        out_shape=(
            jax.ShapeDtypeStruct((2, feat_rows, channels), jnp.float32),
            jax.ShapeDtypeStruct((2, tiles, chunk_rows, channels), jnp.bfloat16),
        ),
        in_specs=[hbm],
        out_specs=(vmem, vmem),
        scratch_shapes=[
            pltpu.VMEM((tiles, part_rows, channels), jnp.float32),
            pltpu.VMEM((tiles, part_rows, channels), jnp.float32),
            pltpu.VMEM((tiles, part_rows, channels), jnp.bfloat16),
            pltpu.VMEM((tiles, part_rows, channels), jnp.bfloat16),
            pltpu.VMEM((2, feat_rows, channels), jnp.float32),
            pltpu.VMEM((2, tiles, chunk_rows, channels), jnp.bfloat16),
            pltpu.SemaphoreType.DMA((2,)),
            pltpu.SemaphoreType.DMA((2, tiles)),
            pltpu.SemaphoreType.DMA((2, tiles)),
            pltpu.SemaphoreType.DMA((2, tiles)),
            pltpu.SemaphoreType.DMA((2,)),
            pltpu.SemaphoreType.DMA,
        ],
        compiler_params=pltpu.CompilerParams(
            collective_id=1, has_side_effects=True, vmem_limit_bytes=(64 << 20) - (380 << 10)
        ),
    )(part)
    feature_grad, weight_grad, bias_grad = pl.pallas_call(
        functools.partial(finish_kernel, 3 * stacked),
        out_shape=(
            jax.ShapeDtypeStruct((rows, channels), jnp.float32),
            jax.ShapeDtypeStruct((3 * stacked, channels), jnp.float32),
            jax.ShapeDtypeStruct((1, out_channels), jnp.float32),
        ),
        in_specs=[vmem, vmem],
        out_specs=(vmem, vmem, vmem),
        compiler_params=pltpu.CompilerParams(vmem_limit_bytes=64 << 20),
    )(feature_grad, sums)
    return (
        prediction,
        feature_grad,
        weight_grad.reshape(weight.shape),
        bias_grad.reshape(out_channels),
    )


def solution(mesh):
    in_specs = (
        P(("groups", "tile"), None),
        P(),
        P(),
        P(("groups", "tile")),
        P("groups"),
        P(("groups", "tile"), None, "sub", None),
    )
    out_specs = (
        P(("groups", "tile"), None, "sub", None),
        P(("groups", "tile"), None),
        P("groups", None, None, None),
        P("groups"),
    )
    return jax.shard_map(
        functools.partial(on_device, mesh.shape["tile"], mesh.shape["sub"]),
        mesh=mesh, in_specs=in_specs, out_specs=out_specs, check_vma=False,
    )
```
